32 devices in a mesh: lat: 8 (over y, x, core), lon: 4 (over z).
Axes of the slice: x: 2, y: 2, z: 4, core: 2. Of those that a mesh axis runs over, the one named last changes fastest.
Arguments:
- fields: bfloat16 [4, 64, 256, 640], P(None, 'lat', 'lon'), may hold values from -6 to 6
- kernel: float32 [64, 9, 3, 256], P('lat'), may hold values from -0.125 to 0.125
- theta: float32 [3, 640], P(None, 'lon'), may hold values from -4 to 4
- row_start: int32 [64], P('lat'), may hold values from 0 to 59, as said below
- row_count: int32 [64], P('lat'), may hold values from 1 to 9
- norm_gain: float32 [640], replicated, may hold values from 0.1 to 1.9
- w_in: bfloat16 [640, 1280], replicated, may hold values from -0.25 to 0.25
- b_in: float32 [1280], replicated, may hold values from -3 to 3
- w_out: bfloat16 [1280, 640], replicated, may hold values from -0.15625 to 0.15625
Outputs:
- block_out: bfloat16 [4, 64, 256, 640], P(None, 'lat', 'lon')
The draws below stay inside these ranges and needn't reach their ends.
Inputs may be any that keep to these rules, and one draw needn't show every extreme that they name: Output row i draws on rows row_start[i] to row_start[i] + row_count[i] - 1, all inside the grid and within 4 rows of i.
All inputs are finite; a program needn't handle non-finite values.
Results may differ from the reference program's by a relative error of at most 0.0085.
Values may be sent and summed in bfloat16 or wider, within the bound.
A program may use at most 192 MiB of HBM per device.

```python
import jax
import jax.numpy as jnp
from jax import lax

C = 640
HID = 1280
KBASIS = 3
REACH = 4
SLOTS = 9
ENS = 4
LAT_DEV = 8
NLAT = 64
NLON = 256


def support_rows(key):
    position = jnp.arange(NLAT, dtype=jnp.int32)
    lowest = jnp.maximum(position - REACH, 0)
    highest = jnp.minimum(position + REACH + 1, NLAT)
    counts = jax.random.randint(jax.random.fold_in(key, 11), (NLAT,), 1, SLOTS + 1)
    offsets = jax.random.randint(jax.random.fold_in(key, 12), (NLAT,), 0, SLOTS)
    offsets = offsets % (SLOTS - counts + 1)
    starts = position - REACH + offsets
    polar = (position < LAT_DEV) | (position >= NLAT - LAT_DEV)
    starts = jnp.where(polar, lowest, starts)
    counts = jnp.where(polar, highest - lowest, counts)
    return (starts.astype(jnp.int32), counts.astype(jnp.int32))


def draw_row_start(key, part):
    return support_rows(key)[0]


def draw_row_count(key, part):
    return support_rows(key)[1]


def shard_levels(stream_key, dims, shards, smallest, top_value):
    def one(dim, blocks):
        steps = jax.random.uniform(jax.random.fold_in(jax.random.fold_in(stream_key, 6), dim), (blocks,), jnp.float32, smallest / len(shards), top_value / len(shards))
        return jnp.repeat(jnp.exp(steps), dims[dim] // blocks).reshape((-1,) + (1,) * (len(dims) - dim - 1))

    level = one(*shards[0])
    for cut in shards[1:]:
        level = level * one(*cut)
    return level


def centred(stream_key, dims, deviation, bound, split=(), kind=jnp.bfloat16):
    loudness = shard_levels(stream_key, dims, split, -0.22, 0.18) if split else 1.0
    entries = jax.random.normal(stream_key, dims, jnp.float32) * deviation * loudness
    return jnp.minimum(jnp.maximum(entries, -bound), bound).astype(kind)


def setup_inputs(seed: int = 0) -> dict:
    key_of = jax.random.split(jax.random.key(seed), 10)
    return {
        "fields": centred(key_of[0], (ENS, NLAT, NLON, C), 1.0, 6.0, ((1, 8), (2, 4))),
        "kernel": centred(key_of[1], (NLAT, SLOTS, KBASIS, NLON), (NLON * SLOTS) ** -0.5, 0.125, ((0, 8),), jnp.float32),
        "theta": centred(key_of[2], (KBASIS, C), 1.0, 4.0, ((1, 4),), jnp.float32),
        "row_start": draw_row_start(jax.random.fold_in(key_of[9], 71), 0),
        "row_count": draw_row_count(jax.random.fold_in(key_of[9], 71), 0),
        "norm_gain": jnp.clip(1.0 + 0.18 * jax.random.normal(key_of[5], (C,), jnp.float32), 0.1, 1.9),
        "w_in": centred(key_of[6], (C, HID), C ** -0.5, 0.25),
        "b_in": centred(key_of[7], (HID,), 0.5, 3.0, (), jnp.float32),
        "w_out": centred(key_of[8], (HID, C), HID ** -0.5, 0.15625),
    }


def conv_member(member, kernel_hat, theta, row_start, row_count):
    spectrum = jnp.fft.fft(member.astype(jnp.float32), axis=1)
    total = jnp.zeros(spectrum.shape, spectrum.dtype)
    for slot in range(SLOTS):
        mixed = jnp.einsum('ikf,kc->ifc', kernel_hat[:, slot], theta)
        source = jnp.clip(row_start + slot, 0, NLAT - 1).astype(jnp.int32)
        live = (slot < row_count)[:, None, None]
        total = total + jnp.where(live, mixed * spectrum[source], jnp.zeros_like(total))
    return jnp.real(jnp.fft.ifft(total, axis=1)).astype(jnp.bfloat16)

def mlp_member(pair, norm_gain, w_in, b_in, w_out):
    member, conv = pair
    values = conv.astype(jnp.float32)
    mean = lax.optimization_barrier(jnp.mean(values, axis=-1, keepdims=True))
    var = lax.optimization_barrier(jnp.mean((values - mean) ** 2, axis=-1, keepdims=True))
    normed = ((values - mean) * lax.rsqrt(var + 1e-05) * norm_gain).astype(jnp.bfloat16)
    hidden = jax.nn.gelu(jnp.einsum('alc,ch->alh', normed.astype(jnp.float32), w_in.astype(jnp.float32)) + b_in, approximate=False).astype(jnp.bfloat16)
    branch = jnp.einsum('alh,hc->alc', hidden.astype(jnp.float32), w_out.astype(jnp.float32))
    return (member.astype(jnp.float32) + branch).astype(jnp.bfloat16)

def reference(fields, kernel, theta, row_start, row_count, norm_gain, w_in, b_in, w_out):
    kernel_hat = jnp.fft.fft(kernel, axis=3)
    conv = lax.map(lambda member: conv_member(member, kernel_hat, theta, row_start, row_count), fields)
    return lax.map(lambda pair: mlp_member(pair, norm_gain, w_in, b_in, w_out), (fields, conv))
```

```python
import functools
import math

import jax
import jax.numpy as jnp
from jax import lax
from jax.experimental import pallas as pl
from jax.experimental.pallas import tpu as pltpu
from jax.sharding import PartitionSpec as P

REACH = 4
WINDOW = 2 * REACH + 1
LANES = 128
MESH = pl.DeviceIdType.MESH


def block_kernel(
    L, T, members, fields, theta, kern_hbm, starts_hbm, counts_hbm, gain_hbm, w_in_hbm, b_in_hbm, w_out_hbm, out,
    wide_a, wide_b, base, taps, kern, starts, counts, gain, w_in, b_in, w_out, theta_buf,
    staged_a, staged_b, got_a, got_b, held,
    send_sem, recv_sem, halo_send, halo_recv, th_send, th_recv, local_sem, a_send, a_recv, b_send, b_recv,
):
    lat, lon = lax.axis_index("lat"), lax.axis_index("lon")
    up, down = lax.rem(lat + 1, T), lax.rem(lat + T - 1, T)
    has_up, has_down = lat < T - 1, lat > 0
    ens, rows, cols, chans = held.shape
    circle = wide_a.shape[2]
    slots, basis = kern.shape[:2]
    head = wide_a.shape[3]
    blocks = circle // LANES

    pairs = ((kern_hbm, kern), (starts_hbm, starts), (counts_hbm, counts), (gain_hbm, gain),
             (w_in_hbm, w_in), (b_in_hbm, b_in), (w_out_hbm, w_out), (fields, held), (theta, theta_buf.at[lon]))
    loads = [pltpu.make_async_copy(a, b, local_sem.at[n]) for n, (a, b) in enumerate(pairs)]
    for copy in loads[:3]:
        copy.start()
    barrier = pltpu.get_barrier_semaphore()
    for step in range(1, L):
        pl.semaphore_signal(barrier, inc=1, device_id={"lon": lax.rem(lon + step, L)}, device_id_type=MESH)
    for other in (up, down):
        pl.semaphore_signal(barrier, inc=1, device_id={"lat": other}, device_id_type=MESH)
    pl.semaphore_wait(barrier, L + 1)

    def lons(owner):
        return pl.ds(pl.multiple_of(owner * cols, cols), cols)

    def member(owner):
        return pl.ds(owner * members, members)

    shared = []
    for step in range(1, L):
        shared.append(pltpu.make_async_remote_copy(
            src_ref=theta, dst_ref=theta_buf.at[lon],
            send_sem=th_send.at[step], recv_sem=th_recv.at[step],
            device_id={"lon": lax.rem(lon + step, L)}, device_id_type=MESH))
        shared[-1].start()
    parts = [(wide_a, pl.ds(0, head), 0, rows), (wide_b, pl.ds(head, chans - head), 0, REACH)]
    if rows > REACH:
        parts.append((wide_b, pl.ds(head, chans - head), REACH, rows - REACH))
    sends = []
    for c, (wide, chan, low, size) in enumerate(parts):
        row = []
        for step in range(1, L):
            peer = lax.rem(lon + step, L)
            row.append(pltpu.make_async_remote_copy(
                src_ref=fields.at[member(peer), pl.ds(low, size), :, chan],
                dst_ref=wide.at[:, pl.ds(REACH + low, size), lons(lon), :],
                send_sem=send_sem.at[c, step], recv_sem=recv_sem.at[c, step],
                device_id={"lon": peer}, device_id_type=MESH))
            row[-1].start()
        sends.append(row)
    mine = [
        pltpu.make_async_copy(
            fields.at[member(lon), :, :, chan], wide.at[:, pl.ds(REACH, rows), lons(lon), :], local_sem.at[len(pairs) + n])
        for n, (wide, chan, _, _) in enumerate(parts[:2])]
    for copy in mine + loads[3:]:
        copy.start()

    def forward(side, part, step, owner):
        wide, chan = parts[part][:2]
        source, target, other, there = ((0, REACH + rows, down, has_down), (rows - REACH, 0, up, has_up))[side]
        if step:
            src = wide.at[:, pl.ds(REACH + source, REACH), lons(owner), :]
        else:
            src = fields.at[member(owner), pl.ds(source, REACH), :, chan]
        copy = pltpu.make_async_remote_copy(
            src_ref=src, dst_ref=wide.at[:, pl.ds(target, REACH), lons(owner), :],
            send_sem=halo_send.at[side, part, step], recv_sem=halo_recv.at[side, part, step],
            device_id={"lat": other}, device_id_type=MESH)
        pl.when(there)(copy.start)
        return copy

    def arrived(side, copies):
        @pl.when((has_up, has_down)[side])
        def _():
            for copy in copies:
                copy.wait_recv()

    owners = [lax.rem(lon + L - step, L) for step in range(L)]
    halo = [[[forward(side, part, 0, lon)] for part in range(2)] for side in range(2)]

    @pl.when(lat == 0)
    def _():
        for wide in (wide_a, wide_b):
            wide[:, :REACH] = jnp.zeros_like(wide[:, :REACH])

    @pl.when(lat == T - 1)
    def _():
        for wide in (wide_a, wide_b):
            wide[:, REACH + rows:] = jnp.zeros_like(wide[:, REACH + rows:])

    place = lax.broadcasted_iota(jnp.int32, (circle, circle), 0) + lax.broadcasted_iota(
        jnp.int32, (circle, circle), 1)
    flip = jnp.where((place == 0) | (place == circle), 1.0, 0.0).astype(jnp.bfloat16)

    for copy in loads[:3]:
        copy.wait()
    profiles = kern[...].reshape(slots * basis * rows, circle).astype(jnp.bfloat16)
    taps[...] = jnp.dot(profiles, flip, preferred_element_type=jnp.float32)

    def build_row(i, carry):
        shift = starts[i] - (lat * rows + i - REACH)
        count = counts[i]
        for w in range(WINDOW):
            slot = w - shift
            live = jnp.where((slot >= 0) & (slot < count), 1.0, 0.0)
            slot = jnp.clip(slot, 0, slots - 1)
            for k in range(basis):
                line = taps[pl.ds((slot * basis + k) * rows + i, 1), :] * live
                turned = pltpu.roll(jnp.broadcast_to(line, (LANES, circle)), 0, 1, stride=1, stride_axis=0)
                base[i, pl.ds(k * LANES, LANES), pl.ds(w * circle, circle)] = turned.astype(jnp.bfloat16)
        return carry

    lax.fori_loop(0, rows, build_row, 0)

    for copy in shared:
        copy.wait_recv()
    loads[8].wait()
    scale = jnp.concatenate([theta_buf[owner] for owner in range(L)], axis=1)

    def window(wide, e, i, h):
        cut = h * LANES
        pieces = []
        for w in range(WINDOW):
            pieces.append(wide[e, i + w, pl.ds(cut, circle - cut), :])
            if cut:
                pieces.append(wide[e, i + w, pl.ds(0, cut), :])
        return jnp.concatenate(pieces, axis=0)

    def mixed(prod, scale):
        total = prod[:LANES] * scale[0:1, :]
        for k in range(1, basis):
            total = total + prod[k * LANES:(k + 1) * LANES] * scale[k:k + 1, :]
        return total.astype(jnp.bfloat16)

    def head_row(slot, carry):
        i = lax.rem(slot + REACH, rows)
        for e in range(members):
            both = jnp.concatenate([window(wide_a, e, i, h) for h in range(blocks)], axis=1)
            prod = jnp.dot(base[i], both, preferred_element_type=jnp.float32)
            for h in range(blocks):
                staged_a[e, slot, pl.ds(h * LANES, LANES), :] = mixed(
                    prod[:, h * head:(h + 1) * head], scale[:, :head])
            got_a[slot, lon * members + e] = staged_a[e, slot, lons(lon), :]
        return carry

    first = max(rows - REACH, 0)
    for step in range(1, L):
        sends[0][step - 1].wait_recv()
        for side in range(2):
            halo[side][0].append(forward(side, 0, step, owners[step]))
    mine[0].wait()
    arrived(0, halo[0][0])
    lax.fori_loop(0, first, head_row, 0)
    arrived(1, halo[1][0])
    lax.fori_loop(first, rows, head_row, 0)

    def back_head(step, e):
        peer = lax.rem(lon + step, L)
        return pltpu.make_async_remote_copy(
            src_ref=staged_a.at[e, :, lons(peer), :], dst_ref=got_a.at[:, lon * members + e],
            send_sem=a_send.at[step, e], recv_sem=a_recv.at[step, e],
            device_id={"lon": peer}, device_id_type=MESH)

    for step in range(1, L):
        for e in range(members):
            back_head(step, e).start()

    for step in range(1, L):
        sends[1][step - 1].wait_recv()
        halo[0][1].append(forward(0, 1, step, owners[step]))
    for step in range(1, L):
        for row in sends[2:]:
            row[step - 1].wait_recv()
        halo[1][1].append(forward(1, 1, step, owners[step]))
    mine[1].wait()
    arrived(0, halo[0][1])

    def back(slot, step, e):
        peer = lax.rem(lon + step, L)
        return pltpu.make_async_remote_copy(
            src_ref=staged_b.at[e, slot, lons(peer), :], dst_ref=got_b.at[slot, lon * members + e],
            send_sem=b_send.at[slot, step, e], recv_sem=b_recv.at[slot, step, e],
            device_id={"lon": peer}, device_id_type=MESH)

    def send_part(slot, h):
        for step in range(1, L):
            peer = lax.rem(lon + step, L)

            @pl.when((peer * cols + cols - 1) // LANES == h)
            def _():
                for e in range(members):
                    back(slot, step, e).start()

    def conv_row(slot, carry):
        i = lax.rem(slot + REACH, rows)
        for e in range(members):
            for h in range(blocks):
                prod = jnp.dot(base[i], window(wide_b, e, i, h), preferred_element_type=jnp.float32)
                staged_b[e, slot, pl.ds(h * LANES, LANES), :] = mixed(prod, scale[:, head:])
                if e == members - 1 and h > 0:
                    send_part(slot, h - 1)
                if e == 0 and h == 0:
                    @pl.when(slot > 0)
                    def _():
                        send_part(slot - 1, blocks - 1)
            got_b[slot, lon * members + e] = staged_b[e, slot, lons(lon), :]
        return carry

    lax.fori_loop(0, first, conv_row, 0)
    arrived(1, halo[1][1])
    lax.fori_loop(first, rows, conv_row, 0)
    for copy in loads[3:8]:
        copy.wait()
    for step in range(1, L):
        for e in range(members):
            back_head(step, e).wait_recv()

    def mlp_row(slot, carry):
        i = lax.rem(slot + REACH, rows)
        for e in range(members):
            for step in range(1, L):
                back(slot, step, e).wait_recv()
        values = jnp.concatenate(
            [got_a[slot].reshape(ens * cols, head), got_b[slot].reshape(ens * cols, chans - head)], axis=1)
        values = values.astype(jnp.float32)
        mean = jnp.mean(values, axis=-1, keepdims=True)
        diff = values - mean
        var = jnp.mean(diff * diff, axis=-1, keepdims=True)
        normed = (diff * lax.rsqrt(var + 1e-05) * gain[...][None, :]).astype(jnp.bfloat16)
        hidden = jnp.dot(normed, w_in[...], preferred_element_type=jnp.float32) + b_in[...][None, :]
        hidden = (0.5 * hidden * (1.0 + lax.erf(hidden * math.sqrt(0.5)))).astype(jnp.bfloat16)

        @pl.when(slot == 0)
        def _():
            send_part(rows - 1, blocks - 1)

        branch = jnp.dot(hidden, w_out[...], preferred_element_type=jnp.float32)
        start = held[:, i].reshape(ens * cols, chans).astype(jnp.float32)
        out[:, i] = (start + branch).astype(jnp.bfloat16).reshape(ens, cols, chans)
        return carry

    lax.fori_loop(0, rows, mlp_row, 0)
    for row in sends:
        for copy in row:
            copy.wait_send()
    for copy in shared:
        copy.wait_send()
    for side in range(2):
        @pl.when((has_down, has_up)[side])
        def _():
            for part in halo[side]:
                for copy in part:
                    copy.wait_send()
    for step in range(1, L):
        for e in range(members):
            back_head(step, e).wait_send()
            for slot in range(rows):
                back(slot, step, e).wait_send()


def block(fields, theta, kern, starts, counts, gain, w_in, b_in, w_out, L, T):
    ens, rows, cols, chans = fields.shape
    members, circle = ens // L, cols * L
    basis = theta.shape[0]
    head = LANES
    tail = chans - head
    dma = pltpu.SemaphoreType.DMA
    bf16 = jnp.bfloat16
    return pl.pallas_call(
        functools.partial(block_kernel, L, T, members),
        out_shape=pltpu.VMEM(fields.shape, bf16),
        in_specs=[pl.BlockSpec(memory_space=pltpu.HBM)] * 9,
        out_specs=pl.BlockSpec(memory_space=pltpu.VMEM),
        scratch_shapes=[
            pltpu.VMEM((members, rows + 2 * REACH, circle, head), bf16),
            pltpu.VMEM((members, rows + 2 * REACH, circle, tail), bf16),
            pltpu.VMEM((rows, basis * LANES, WINDOW * circle), bf16),
            pltpu.VMEM((kern.shape[0] * basis * rows, circle), jnp.float32),
            pltpu.VMEM(kern.shape, jnp.float32),
            pltpu.SMEM(starts.shape, jnp.int32),
            pltpu.SMEM(counts.shape, jnp.int32),
            pltpu.VMEM(gain.shape, jnp.float32),
            pltpu.VMEM(w_in.shape, bf16),
            pltpu.VMEM(b_in.shape, jnp.float32),
            pltpu.VMEM(w_out.shape, bf16),
            pltpu.VMEM((L,) + theta.shape, jnp.float32),
            pltpu.VMEM((members, rows, circle, head), bf16),
            pltpu.VMEM((members, rows, circle, tail), bf16),
            pltpu.VMEM((rows, ens, cols, head), bf16),
            pltpu.VMEM((rows, ens, cols, tail), bf16),
            pltpu.VMEM(fields.shape, bf16),
            dma((3, L)), dma((3, L)), dma((2, 2, L)), dma((2, 2, L)), dma((L,)), dma((L,)), dma((11,)),
            dma((L, members)), dma((L, members)), dma((rows, L, members)), dma((rows, L, members)),
        ],
        compiler_params=pltpu.CompilerParams(
            collective_id=0, has_side_effects=True, vmem_limit_bytes=52 * 2**20),
        name="block",
    )(fields, theta, kern, starts, counts, gain, w_in, b_in, w_out)


def with_halo(value, sides, width):
    for axis, dim in sides:
        size, length = (lax.axis_size(axis), value.shape[dim])
        up = [(i, (i + 1) % size) for i in range(size - 1)]
        down = [(j, i) for i, j in up]
        last = lax.slice_in_dim(value, length - width, length, axis=dim)
        initial = lax.slice_in_dim(value, 0, width, axis=dim)
        before = lax.ppermute(last, axis, up)
        after = lax.ppermute(initial, axis, down)
        value = jnp.concatenate([before, value, after], axis=dim)
    return value


def circle_tables(length):
    bins = length // 2 + 1
    points = jnp.arange(length, dtype=jnp.int32)
    freqs = jnp.arange(bins, dtype=jnp.int32)
    phase = points[:, None] * freqs[None, :] % length
    angle = phase.astype(jnp.float32) * (2.0 * math.pi / length)
    cosine = jnp.cos(angle)
    sine = jnp.sin(angle)
    onward = jnp.concatenate([cosine, -sine], axis=1)
    weight = jnp.where((freqs == 0) | (freqs == length // 2), 1.0, 2.0).astype(jnp.float32)
    backward = (
        jnp.concatenate([(cosine * weight[None, :]).T, (-sine * weight[None, :]).T], axis=0)
        / length
    )
    return (onward, backward, bins)


def forward(field, onward, bins):
    upper = onward.astype(jnp.bfloat16)
    lower = (onward - upper.astype(jnp.float32)).astype(jnp.bfloat16)
    spectrum = jnp.einsum("ejlc,lg->ejgc", field, upper, preferred_element_type=jnp.float32)
    spectrum = spectrum + jnp.einsum(
        "ejlc,lg->ejgc", field, lower, preferred_element_type=jnp.float32
    )
    return (spectrum[:, :, :bins], spectrum[:, :, bins:])


def mix_basis(kern_part, theta):
    mixed = kern_part[:, :, 0, :, None] * theta[0][None, None, None, :]
    for basis in range(1, kern_part.shape[2]):
        mixed = mixed + kern_part[:, :, basis, :, None] * theta[basis][None, None, None, :]
    return mixed


def spectral_shards(fields, kernel, theta, row_start, row_count, norm_gain, w_in, b_in, w_out):
    local = lax.all_to_all(fields, "lon", split_axis=3, concat_axis=2, tiled=True)
    members, band, circle, chans = local.shape
    onward, backward, bins = circle_tables(circle)
    widened = with_halo(local, (("lat", 1),), REACH)
    spec_re, spec_im = forward(widened, onward, bins)
    kern_all = jnp.einsum("irkm,mg->irkg", kernel, onward, precision=lax.Precision.HIGHEST)
    mixed_re = mix_basis(kern_all[..., :bins], theta)
    mixed_im = mix_basis(kern_all[..., bins:], theta)
    first_row = lax.axis_index("lat") * band - REACH
    span_rows = band + 2 * REACH
    slot_ids = jnp.arange(WINDOW, dtype=jnp.int32)
    offsets = row_start - first_row
    live_slot = slot_ids[None, :] < row_count[:, None]
    total_re = jnp.zeros((members, band, bins, chans), jnp.float32)
    total_im = jnp.zeros((members, band, bins, chans), jnp.float32)
    for span in range(span_rows):
        select = (live_slot & (offsets[:, None] + slot_ids[None, :] == span)).astype(jnp.float32)
        coef_re = jnp.einsum("is,isfc->ifc", select, mixed_re, precision=lax.Precision.HIGHEST)
        coef_im = jnp.einsum("is,isfc->ifc", select, mixed_im, precision=lax.Precision.HIGHEST)
        row_re = spec_re[:, span][:, None]
        row_im = spec_im[:, span][:, None]
        total_re = total_re + coef_re * row_re - coef_im * row_im
        total_im = total_im + coef_re * row_im + coef_im * row_re
    joined = jnp.concatenate([total_re, total_im], axis=2)
    conv = jnp.einsum("eigc,gl->eilc", joined, backward, precision=lax.Precision.HIGHEST).astype(
        jnp.bfloat16
    )
    values = lax.all_to_all(conv, "lon", split_axis=2, concat_axis=3, tiled=True).astype(
        jnp.float32
    )
    mean = jnp.mean(values, axis=-1, keepdims=True)
    var = jnp.mean((values - mean) ** 2, axis=-1, keepdims=True)
    normed = ((values - mean) * lax.rsqrt(var + 1e-05) * norm_gain).astype(jnp.bfloat16)
    hidden = jax.nn.gelu(
        jnp.einsum("eblc,ch->eblh", normed, w_in, preferred_element_type=jnp.float32) + b_in,
        approximate=False,
    ).astype(jnp.bfloat16)
    branch = jnp.einsum("eblh,hc->eblc", hidden, w_out, preferred_element_type=jnp.float32)
    return (fields.astype(jnp.float32) + branch).astype(jnp.bfloat16)


def shards(L, T, fields, kernel, theta, row_start, row_count, norm_gain, w_in, b_in, w_out):
    if fields.shape[0] % L:
        return spectral_shards(
            fields, kernel, theta, row_start, row_count, norm_gain, w_in, b_in, w_out
        )
    kern = jnp.transpose(kernel, (1, 2, 0, 3))
    return block(fields, theta, kern, row_start, row_count, norm_gain, w_in, b_in, w_out, L, T)


def solution(mesh):
    placed = (
        P(None, "lat", "lon", None),
        P("lat", None, None, None),
        P(None, "lon"),
        P("lat"),
        P("lat"),
        P(),
        P(),
        P(),
        P(),
    )
    return jax.shard_map(
        functools.partial(shards, mesh.shape["lon"], mesh.shape["lat"]),
        mesh=mesh, in_specs=placed, out_specs=P(None, "lat", "lon", None), check_vma=False,
    )
```

```python
import functools
import math

import jax
import jax.numpy as jnp
from jax import lax
from jax.experimental import pallas as pl
from jax.experimental.pallas import tpu as pltpu
from jax.sharding import PartitionSpec as P

REACH = 4
WINDOW = 2 * REACH + 1
LANES = 128
MESH = pl.DeviceIdType.MESH


def block_kernel(
    L, T, members, fields, theta, kern_hbm, starts_hbm, counts_hbm, gain_hbm, w_in_hbm, b_in_hbm, w_out_hbm, out,
    wide_a, wide_b, base, taps, kern, starts, counts, gain, w_in, b_in, w_out, theta_buf,
    staged_a, staged_b, got_a, got_b, held,
    send_sem, recv_sem, halo_send, halo_recv, th_sem, local_sem, back_send, a_recv, b_recv,
):
    lat, lon = lax.axis_index("lat"), lax.axis_index("lon")
    up, down = lax.rem(lat + 1, T), lax.rem(lat + T - 1, T)
    has_up, has_down = lat < T - 1, lat > 0
    ens, rows, cols, chans = held.shape
    circle = wide_a.shape[2]
    slots, basis = kern.shape[:2]
    head = wide_a.shape[3]
    blocks = circle // LANES

    pairs = ((kern_hbm, kern), (starts_hbm, starts), (counts_hbm, counts), (gain_hbm, gain),
             (w_in_hbm, w_in), (b_in_hbm, b_in), (w_out_hbm, w_out), (fields, held), (theta, theta_buf.at[lon]))
    loads = [pltpu.make_async_copy(a, b, local_sem.at[n]) for n, (a, b) in enumerate(pairs)]
    for copy in loads[:3]:
        copy.start()
    barrier = pltpu.get_barrier_semaphore()
    for step in range(1, L):
        pl.semaphore_signal(barrier, inc=1, device_id={"lon": lax.rem(lon + step, L)}, device_id_type=MESH)
    for other in (up, down):
        pl.semaphore_signal(barrier, inc=1, device_id={"lat": other}, device_id_type=MESH)
    pl.semaphore_wait(barrier, L + 1)

    def lons(owner):
        return pl.ds(pl.multiple_of(owner * cols, cols), cols)

    def member(owner):
        return pl.ds(owner * members, members)

    for step in range(1, L):
        pltpu.make_async_remote_copy(
            src_ref=theta, dst_ref=theta_buf.at[lon],
            send_sem=th_sem.at[0], recv_sem=th_sem.at[1],
            device_id={"lon": lax.rem(lon + step, L)}, device_id_type=MESH).start()
    parts = [(wide_a, pl.ds(0, head), 0, rows), (wide_b, pl.ds(head, chans - head), 0, REACH)]
    if rows > REACH:
        parts.append((wide_b, pl.ds(head, chans - head), REACH, rows - REACH))
    sends = []
    for c, (wide, chan, low, size) in enumerate(parts):
        row = []
        for step in range(1, L):
            peer = lax.rem(lon + step, L)
            row.append(pltpu.make_async_remote_copy(
                src_ref=fields.at[member(peer), pl.ds(low, size), :, chan],
                dst_ref=wide.at[:, pl.ds(REACH + low, size), lons(lon), :],
                send_sem=send_sem.at[0], recv_sem=recv_sem.at[c, step - 1],
                device_id={"lon": peer}, device_id_type=MESH))
            row[-1].start()
        sends.append(row)
    mine = [
        pltpu.make_async_copy(
            fields.at[member(lon), :, :, chan], wide.at[:, pl.ds(REACH, rows), lons(lon), :], local_sem.at[len(pairs) + n])
        for n, (wide, chan, _, _) in enumerate(parts[:2])]
    for copy in mine + loads[3:]:
        copy.start()

    def forward(side, part, step, owner):
        wide, chan = parts[part][:2]
        source, target, other, there = ((0, REACH + rows, down, has_down), (rows - REACH, 0, up, has_up))[side]
        if step:
            src = wide.at[:, pl.ds(REACH + source, REACH), lons(owner), :]
        else:
            src = fields.at[member(owner), pl.ds(source, REACH), :, chan]
        copy = pltpu.make_async_remote_copy(
            src_ref=src, dst_ref=wide.at[:, pl.ds(target, REACH), lons(owner), :],
            send_sem=halo_send.at[side, part], recv_sem=halo_recv.at[side, part],
            device_id={"lat": other}, device_id_type=MESH)
        pl.when(there)(copy.start)

    def take(ref, sem):
        pltpu.make_async_copy(ref, ref, sem).wait()

    def arrived(side, part):
        @pl.when((has_up, has_down)[side])
        def _():
            target = (REACH + rows, 0)[side]
            take(parts[part][0].at[:, pl.ds(target, REACH)], halo_recv.at[side, part])

    owners = [lax.rem(lon + L - step, L) for step in range(L)]
    for side in range(2):
        for part in range(2):
            forward(side, part, 0, lon)

    @pl.when(lat == 0)
    def _():
        for wide in (wide_a, wide_b):
            wide[:, :REACH] = jnp.zeros_like(wide[:, :REACH])

    @pl.when(lat == T - 1)
    def _():
        for wide in (wide_a, wide_b):
            wide[:, REACH + rows:] = jnp.zeros_like(wide[:, REACH + rows:])

    place = lax.broadcasted_iota(jnp.int32, (circle, circle), 0) + lax.broadcasted_iota(
        jnp.int32, (circle, circle), 1)
    flip = jnp.where((place == 0) | (place == circle), 1.0, 0.0).astype(jnp.bfloat16)

    for copy in loads[:3]:
        copy.wait()
    profiles = kern[...].reshape(slots * basis * rows, circle).astype(jnp.bfloat16)
    taps[...] = jnp.dot(profiles, flip, preferred_element_type=jnp.float32)

    def build_row(i, carry):
        shift = starts[i] - (lat * rows + i - REACH)
        count = counts[i]
        for w in range(WINDOW):
            slot = w - shift
            live = jnp.where((slot >= 0) & (slot < count), 1.0, 0.0)
            slot = jnp.clip(slot, 0, slots - 1)
            for k in range(basis):
                line = taps[pl.ds((slot * basis + k) * rows + i, 1), :] * live
                turned = pltpu.roll(jnp.broadcast_to(line, (LANES, circle)), 0, 1, stride=1, stride_axis=0)
                base[i, pl.ds(k * LANES, LANES), pl.ds(w * circle, circle)] = turned.astype(jnp.bfloat16)
        return carry

    lax.fori_loop(0, rows, build_row, 0)

    take(theta_buf.at[pl.ds(0, L - 1)], th_sem.at[1])
    loads[8].wait()
    scale = jnp.concatenate([theta_buf[owner] for owner in range(L)], axis=1)

    def window(wide, e, i, h):
        cut = h * LANES
        pieces = []
        for w in range(WINDOW):
            pieces.append(wide[e, i + w, pl.ds(cut, circle - cut), :])
            if cut:
                pieces.append(wide[e, i + w, pl.ds(0, cut), :])
        return jnp.concatenate(pieces, axis=0)

    def mixed(prod, scale):
        total = prod[:LANES] * scale[0:1, :]
        for k in range(1, basis):
            total = total + prod[k * LANES:(k + 1) * LANES] * scale[k:k + 1, :]
        return total.astype(jnp.bfloat16)

    latest = jnp.where(lon < L // 2, L // 2, L // 2 - 1)

    def place_of(source, target):
        return lax.rem(source + L - (L // 2 if target < L // 2 else L // 2 - 1), L)

    def head_row(slot, carry):
        i = lax.rem(slot + REACH, rows)
        for e in range(members):
            both = jnp.concatenate([window(wide_a, e, i, h) for h in range(blocks)], axis=1)
            prod = jnp.dot(base[i], both, preferred_element_type=jnp.float32)
            for h in range(blocks):
                staged_a[e, slot, pl.ds(h * LANES, LANES), :] = mixed(
                    prod[:, h * head:(h + 1) * head], scale[:, :head])
            got_a[slot, lax.rem(lon + L - latest, L) * members + e] = staged_a[e, slot, lons(lon), :]
        return carry

    first = max(rows - REACH, 0)
    for step in range(1, L):
        sends[0][step - 1].wait_recv()
        for side in range(2):
            forward(side, 0, step, owners[step])
    mine[0].wait()
    arrived(0, 0)
    lax.fori_loop(0, first, head_row, 0)
    arrived(1, 0)
    lax.fori_loop(first, rows, head_row, 0)

    def back_head(target, e):
        return pltpu.make_async_remote_copy(
            src_ref=staged_a.at[e, :, lons(target), :], dst_ref=got_a.at[:, place_of(lon, target) * members + e],
            send_sem=back_send.at[0], recv_sem=a_recv.at[0],
            device_id={"lon": target}, device_id_type=MESH)

    outward = sorted(range(L), key=lambda p: min(p, L - 1 - p))
    for target in outward:
        @pl.when(lon != target)
        def _():
            for e in range(members):
                back_head(target, e).start()

    for step in range(1, L):
        sends[1][step - 1].wait_recv()
        forward(0, 1, step, owners[step])
    for step in range(1, L):
        for row in sends[2:]:
            row[step - 1].wait_recv()
        forward(1, 1, step, owners[step])
    mine[1].wait()
    arrived(0, 1)

    def back(slot, target, e, late):
        return pltpu.make_async_remote_copy(
            src_ref=staged_b.at[e, slot, lons(target), :], dst_ref=got_b.at[slot, place_of(lon, target) * members + e],
            send_sem=back_send.at[0], recv_sem=b_recv.at[slot, 0 if late else 1],
            device_id={"lon": target}, device_id_type=MESH)

    def send_one(slot, target):
        last = L // 2 if target < L // 2 else L // 2 - 1
        for late in (False, True):
            @pl.when((lon == last) if late else (lon != target) & (lon != last))
            def _():
                for e in range(members):
                    back(slot, target, e, late).start()

    def send_part(slot, h):
        for target in outward:
            if (target * cols + cols - 1) // LANES == h:
                send_one(slot, target)

    def conv_row(slot, carry):
        i = lax.rem(slot + REACH, rows)
        for e in range(members):
            for h in range(blocks):
                prod = jnp.dot(base[i], window(wide_b, e, i, h), preferred_element_type=jnp.float32)
                staged_b[e, slot, pl.ds(h * LANES, LANES), :] = mixed(prod, scale[:, head:])
                if e == members - 1 and h > 0:
                    send_part(slot, h - 1)
                if e == 0 and h == 0:
                    @pl.when(slot > 0)
                    def _():
                        send_part(slot - 1, blocks - 1)
            got_b[slot, lax.rem(lon + L - latest, L) * members + e] = staged_b[e, slot, lons(lon), :]
        return carry

    lax.fori_loop(0, first, conv_row, 0)
    arrived(1, 1)
    lax.fori_loop(first, rows, conv_row, 0)
    for copy in loads[3:8]:
        copy.wait()
    take(got_a.at[:, pl.ds(0, (L - 1) * members)], a_recv.at[0])

    def mlp_part(slot, low, high):
        i = lax.rem(slot + REACH, rows)
        fresh = (high - low - min(low, 1)) * members
        take(got_b.at[slot, pl.ds(0, fresh)], b_recv.at[slot, min(low, 1)])
        count = (high - low) * members
        here = pl.ds(low * members, count)
        values = jnp.concatenate(
            [got_a[slot, here].reshape(count * cols, head), got_b[slot, here].reshape(count * cols, chans - head)], axis=1)
        values = values.astype(jnp.float32)
        mean = jnp.mean(values, axis=-1, keepdims=True)
        diff = values - mean
        var = jnp.mean(diff * diff, axis=-1, keepdims=True)
        normed = (diff * lax.rsqrt(var + 1e-05) * gain[...][None, :]).astype(jnp.bfloat16)
        hidden = jnp.dot(normed, w_in[...], preferred_element_type=jnp.float32) + b_in[...][None, :]
        hidden = (0.5 * hidden * (1.0 + lax.erf(hidden * math.sqrt(0.5)))).astype(jnp.bfloat16)
        branch = jnp.dot(hidden, w_out[...], preferred_element_type=jnp.float32).reshape(high - low, members, cols, chans)
        for g in range(low, high):
            owned = pl.ds(lax.rem(latest + g, L) * members, members)
            out[owned, i] = (held[owned, i].astype(jnp.float32) + branch[g - low]).astype(jnp.bfloat16)

    def early_row(slot, carry):
        mlp_part(slot, 1, L)

        @pl.when(slot == 0)
        def _():
            send_part(rows - 1, blocks - 1)

        return carry

    def late_row(slot, carry):
        mlp_part(slot, 0, 1)
        return carry

    lax.fori_loop(0, rows, early_row, 0)
    take(held.at[pl.ds(0, (L - 1) * members)], send_sem.at[0])
    take(theta_buf.at[pl.ds(0, L - 1)], th_sem.at[0])
    for side in range(2):
        @pl.when((has_down, has_up)[side])
        def _():
            for part in range(2):
                take(parts[part][0].at[:, pl.ds(0, REACH)], halo_send.at[side, part])
    lax.fori_loop(0, rows, late_row, 0)
    take(held.at[pl.ds(0, (L - 1) * members)], back_send.at[0])


def block(fields, theta, kern, starts, counts, gain, w_in, b_in, w_out, L, T):
    ens, rows, cols, chans = fields.shape
    members, circle = ens // L, cols * L
    basis = theta.shape[0]
    head = LANES
    tail = chans - head
    dma = pltpu.SemaphoreType.DMA
    bf16 = jnp.bfloat16
    return pl.pallas_call(
        functools.partial(block_kernel, L, T, members),
        out_shape=pltpu.VMEM(fields.shape, bf16),
        in_specs=[pl.BlockSpec(memory_space=pltpu.HBM)] * 9,
        out_specs=pl.BlockSpec(memory_space=pltpu.VMEM),
        scratch_shapes=[
            pltpu.VMEM((members, rows + 2 * REACH, circle, head), bf16),
            pltpu.VMEM((members, rows + 2 * REACH, circle, tail), bf16),
            pltpu.VMEM((rows, basis * LANES, WINDOW * circle), bf16),
            pltpu.VMEM((kern.shape[0] * basis * rows, circle), jnp.float32),
            pltpu.VMEM(kern.shape, jnp.float32),
            pltpu.SMEM(starts.shape, jnp.int32),
            pltpu.SMEM(counts.shape, jnp.int32),
            pltpu.VMEM(gain.shape, jnp.float32),
            pltpu.VMEM(w_in.shape, bf16),
            pltpu.VMEM(b_in.shape, jnp.float32),
            pltpu.VMEM(w_out.shape, bf16),
            pltpu.VMEM((L,) + theta.shape, jnp.float32),
            pltpu.VMEM((members, rows, circle, head), bf16),
            pltpu.VMEM((members, rows, circle, tail), bf16),
            pltpu.VMEM((rows, ens, cols, head), bf16),
            pltpu.VMEM((rows, ens, cols, tail), bf16),
            pltpu.VMEM(fields.shape, bf16),
            dma((1,)), dma((3, L - 1)), dma((2, 2)), dma((2, 2)), dma((2,)), dma((11,)), dma((1,)), dma((1,)), dma((rows, 2)),
        ],
        compiler_params=pltpu.CompilerParams(
            collective_id=0, has_side_effects=True, vmem_limit_bytes=52 * 2**20),
        name="block",
    )(fields, theta, kern, starts, counts, gain, w_in, b_in, w_out)


def with_halo(value, sides, width):
    for axis, dim in sides:
        size, length = (lax.axis_size(axis), value.shape[dim])
        up = [(i, (i + 1) % size) for i in range(size - 1)]
        down = [(j, i) for i, j in up]
        last = lax.slice_in_dim(value, length - width, length, axis=dim)
        initial = lax.slice_in_dim(value, 0, width, axis=dim)
        before = lax.ppermute(last, axis, up)
        after = lax.ppermute(initial, axis, down)
        value = jnp.concatenate([before, value, after], axis=dim)
    return value


def circle_tables(length):
    bins = length // 2 + 1
    points = jnp.arange(length, dtype=jnp.int32)
    freqs = jnp.arange(bins, dtype=jnp.int32)
    phase = points[:, None] * freqs[None, :] % length
    angle = phase.astype(jnp.float32) * (2.0 * math.pi / length)
    cosine = jnp.cos(angle)
    sine = jnp.sin(angle)
    onward = jnp.concatenate([cosine, -sine], axis=1)
    weight = jnp.where((freqs == 0) | (freqs == length // 2), 1.0, 2.0).astype(jnp.float32)
    backward = (
        jnp.concatenate([(cosine * weight[None, :]).T, (-sine * weight[None, :]).T], axis=0)
        / length
    )
    return (onward, backward, bins)


def forward(field, onward, bins):
    upper = onward.astype(jnp.bfloat16)
    lower = (onward - upper.astype(jnp.float32)).astype(jnp.bfloat16)
    spectrum = jnp.einsum("ejlc,lg->ejgc", field, upper, preferred_element_type=jnp.float32)
    spectrum = spectrum + jnp.einsum(
        "ejlc,lg->ejgc", field, lower, preferred_element_type=jnp.float32
    )
    return (spectrum[:, :, :bins], spectrum[:, :, bins:])


def mix_basis(kern_part, theta):
    mixed = kern_part[:, :, 0, :, None] * theta[0][None, None, None, :]
    for basis in range(1, kern_part.shape[2]):
        mixed = mixed + kern_part[:, :, basis, :, None] * theta[basis][None, None, None, :]
    return mixed


def spectral_shards(fields, kernel, theta, row_start, row_count, norm_gain, w_in, b_in, w_out):
    local = lax.all_to_all(fields, "lon", split_axis=3, concat_axis=2, tiled=True)
    members, band, circle, chans = local.shape
    onward, backward, bins = circle_tables(circle)
    widened = with_halo(local, (("lat", 1),), REACH)
    spec_re, spec_im = forward(widened, onward, bins)
    kern_all = jnp.einsum("irkm,mg->irkg", kernel, onward, precision=lax.Precision.HIGHEST)
    mixed_re = mix_basis(kern_all[..., :bins], theta)
    mixed_im = mix_basis(kern_all[..., bins:], theta)
    first_row = lax.axis_index("lat") * band - REACH
    span_rows = band + 2 * REACH
    slot_ids = jnp.arange(WINDOW, dtype=jnp.int32)
    offsets = row_start - first_row
    live_slot = slot_ids[None, :] < row_count[:, None]
    total_re = jnp.zeros((members, band, bins, chans), jnp.float32)
    total_im = jnp.zeros((members, band, bins, chans), jnp.float32)
    for span in range(span_rows):
        select = (live_slot & (offsets[:, None] + slot_ids[None, :] == span)).astype(jnp.float32)
        coef_re = jnp.einsum("is,isfc->ifc", select, mixed_re, precision=lax.Precision.HIGHEST)
        coef_im = jnp.einsum("is,isfc->ifc", select, mixed_im, precision=lax.Precision.HIGHEST)
        row_re = spec_re[:, span][:, None]
        row_im = spec_im[:, span][:, None]
        total_re = total_re + coef_re * row_re - coef_im * row_im
        total_im = total_im + coef_re * row_im + coef_im * row_re
    joined = jnp.concatenate([total_re, total_im], axis=2)
    conv = jnp.einsum("eigc,gl->eilc", joined, backward, precision=lax.Precision.HIGHEST).astype(
        jnp.bfloat16
    )
    values = lax.all_to_all(conv, "lon", split_axis=2, concat_axis=3, tiled=True).astype(
        jnp.float32
    )
    mean = jnp.mean(values, axis=-1, keepdims=True)
    var = jnp.mean((values - mean) ** 2, axis=-1, keepdims=True)
    normed = ((values - mean) * lax.rsqrt(var + 1e-05) * norm_gain).astype(jnp.bfloat16)
    hidden = jax.nn.gelu(
        jnp.einsum("eblc,ch->eblh", normed, w_in, preferred_element_type=jnp.float32) + b_in,
        approximate=False,
    ).astype(jnp.bfloat16)
    branch = jnp.einsum("eblh,hc->eblc", hidden, w_out, preferred_element_type=jnp.float32)
    return (fields.astype(jnp.float32) + branch).astype(jnp.bfloat16)


def shards(L, T, fields, kernel, theta, row_start, row_count, norm_gain, w_in, b_in, w_out):
    if fields.shape[0] % L:
        return spectral_shards(
            fields, kernel, theta, row_start, row_count, norm_gain, w_in, b_in, w_out
        )
    kern = jnp.transpose(kernel, (1, 2, 0, 3))
    return block(fields, theta, kern, row_start, row_count, norm_gain, w_in, b_in, w_out, L, T)


def solution(mesh):
    placed = (
        P(None, "lat", "lon", None),
        P("lat", None, None, None),
        P(None, "lon"),
        P("lat"),
        P("lat"),
        P(),
        P(),
        P(),
        P(),
    )
    return jax.shard_map(
        functools.partial(shards, mesh.shape["lon"], mesh.shape["lat"]),
        mesh=mesh, in_specs=placed, out_specs=P(None, "lat", "lon", None), check_vma=False,
    )
```

```python
import functools
import math

import jax
import jax.numpy as jnp
from jax import lax
from jax.experimental import pallas as pl
from jax.experimental.pallas import tpu as pltpu
from jax.sharding import PartitionSpec as P

REACH = 4
WINDOW = 2 * REACH + 1
LANES = 128
BEHIND = 2
MESH = pl.DeviceIdType.MESH


def block_kernel(
    L, T, members, fields, theta, kern_hbm, starts_hbm, counts_hbm, gain_hbm, w_in_hbm, b_in_hbm, w_out_hbm, out,
    wide_a, wide_b, base, taps, kern, starts, counts, gain, w_in, b_in, w_out, theta_buf,
    staged_a, staged_b, got_a, got_b, held,
    far_sem, lat_sem, send_sem, recv_sem, halo_send, halo_recv, th_sem, local_sem, back_send, a_recv, b_recv,
):
    lat, lon = lax.axis_index("lat"), lax.axis_index("lon")
    up, down = lax.rem(lat + 1, T), lax.rem(lat + T - 1, T)
    has_up, has_down = lat < T - 1, lat > 0
    ens, rows, cols, chans = held.shape
    circle = wide_a.shape[2]
    slots, basis = kern.shape[:2]
    head = wide_a.shape[3]
    blocks = circle // LANES

    pairs = ((kern_hbm, kern), (starts_hbm, starts), (counts_hbm, counts), (gain_hbm, gain),
             (w_in_hbm, w_in), (b_in_hbm, b_in), (w_out_hbm, w_out), (fields, held), (theta, theta_buf.at[lon]))
    loads = [pltpu.make_async_copy(a, b, local_sem.at[n]) for n, (a, b) in enumerate(pairs)]
    for copy in loads[:3]:
        copy.start()
    barrier = pltpu.get_barrier_semaphore()
    half = L // 2
    low = lon < half
    inward, outward_by = jnp.where(low, lon + 1, lon - 1), jnp.where(low, lon - 1, lon + 1)
    middle = (lon == half - 1) | (lon == half)
    at_end = (lon == 0) | (lon == L - 1)
    relayed = ((lon == 1) | (lon == L - 2)) if L > 3 else lon < 0
    beside = ((down, has_down), (up, has_up))

    def signal(sem, when, **device):
        @pl.when(when)
        def _():
            pl.semaphore_signal(sem, inc=1, device_id=device, device_id_type=MESH)

    signal(barrier, ~at_end, lon=outward_by)
    signal(barrier, middle, lon=inward)
    for other, there in beside:
        signal(barrier, there & ~relayed, lat=other)
    greeted = [jnp.where(there & ~relayed, 1, 0) for _, there in beside]
    pl.semaphore_wait(barrier, 1 + greeted[0] + greeted[1])

    def learn(side, when):
        @pl.when(when)
        def _():
            pl.semaphore_wait(far_sem.at[side], 1)

    def take(ref, sem):
        pltpu.make_async_copy(ref, ref, sem).wait()

    owners = [lax.rem(lon + L - step, L) for step in range(L)]

    def lons(owner):
        return pl.ds(pl.multiple_of(owner * cols, cols), cols)

    def member(owner):
        return pl.ds(owner * members, members)

    parts = [(wide_a, pl.ds(0, head), 0, rows), (wide_b, pl.ds(head, chans - head), 0, REACH)]
    if rows > REACH:
        parts.append((wide_b, pl.ds(head, chans - head), REACH, rows - REACH))
    def send_theta(peer):
        pltpu.make_async_remote_copy(
            src_ref=theta, dst_ref=theta_buf.at[lon], send_sem=th_sem.at[0], recv_sem=th_sem.at[1],
            device_id={"lon": peer}, device_id_type=MESH).start()

    def outgoing(c, peer):
        wide, chan, low, size = parts[c]
        return pltpu.make_async_remote_copy(
            src_ref=fields.at[member(peer), pl.ds(low, size), :, chan],
            dst_ref=wide.at[:, pl.ds(REACH + low, size), lons(lon), :],
            send_sem=send_sem.at[0], recv_sem=recv_sem.at[c, lax.rem(peer - lon + L, L) - 1],
            device_id={"lon": peer}, device_id_type=MESH)

    def incoming(c, step):
        wide, chan, low, size = parts[c]
        take(wide.at[:, pl.ds(REACH + low, size), lons(owners[step]), :], recv_sem.at[c, step - 1])

    def both_ways(distance, act):
        for peer, known in ((lon - distance, lon >= distance), (lon + distance, lon + distance < L)):
            pl.when(known)(functools.partial(act, peer))

    def begin(peer):
        send_theta(peer)
        outgoing(0, peer).start()

    signal(far_sem.at[1], ~middle, lon=inward)
    begin(inward)
    for side, (other, there) in enumerate(beside):
        signal(lat_sem.at[1 - side], there & at_end & (L > 3), lat=other)
    inner_count = jnp.where(low, L - 1 - lon, lon)
    outer_count = L - 1 - inner_count
    for distance in range(1, L):
        known = distance <= outer_count
        learn(1, known)
        signal(far_sem.at[1], known & ~middle, lon=inward)
        if distance == 1:
            signal(far_sem.at[0], known, lon=outward_by)
            signal(far_sem.at[0], known & middle, lon=inward)
        else:
            signal(far_sem.at[0], known & middle, lon=inward)
        pl.when(known)(functools.partial(begin, jnp.where(low, lon - distance, lon + distance)))
        if distance > 1:
            known = distance <= inner_count
            learn(0, known)
            signal(far_sem.at[0], known & ~at_end, lon=outward_by)
            pl.when(known)(functools.partial(begin, jnp.where(low, lon + distance, lon - distance)))
    for side, (other, there) in enumerate(beside):
        @pl.when(there & (at_end | relayed) & (L > 3))
        def _():
            pl.semaphore_wait(lat_sem.at[side], 1)

        signal(lat_sem.at[side], there & at_end & (L > 3), lon=inward)
    for c in range(1, len(parts)):
        for distance in range(1, L):
            both_ways(distance, lambda peer: outgoing(c, peer).start())
    mine = [
        pltpu.make_async_copy(
            fields.at[member(lon), :, :, chan], wide.at[:, pl.ds(REACH, rows), lons(lon), :], local_sem.at[len(pairs) + n])
        for n, (wide, chan, _, _) in enumerate(parts[:2])]
    for copy in mine + loads[3:]:
        copy.start()

    def forward(side, part, step, owner):
        wide, chan = parts[part][:2]
        source, target, other, there = ((0, REACH + rows, down, has_down), (rows - REACH, 0, up, has_up))[side]
        if step:
            src = wide.at[:, pl.ds(REACH + source, REACH), lons(owner), :]
        else:
            src = fields.at[member(owner), pl.ds(source, REACH), :, chan]
        copy = pltpu.make_async_remote_copy(
            src_ref=src, dst_ref=wide.at[:, pl.ds(target, REACH), lons(owner), :],
            send_sem=halo_send.at[side, part], recv_sem=halo_recv.at[side, part],
            device_id={"lat": other}, device_id_type=MESH)
        pl.when(there)(copy.start)

    def arrived(side, part):
        @pl.when((has_up, has_down)[side])
        def _():
            target = (REACH + rows, 0)[side]
            take(parts[part][0].at[:, pl.ds(target, REACH)], halo_recv.at[side, part])

    for side in range(2):
        for part in range(2):
            forward(side, part, 0, lon)

    @pl.when(lat == 0)
    def _():
        for wide in (wide_a, wide_b):
            wide[:, :REACH] = jnp.zeros_like(wide[:, :REACH])

    @pl.when(lat == T - 1)
    def _():
        for wide in (wide_a, wide_b):
            wide[:, REACH + rows:] = jnp.zeros_like(wide[:, REACH + rows:])

    place = lax.broadcasted_iota(jnp.int32, (circle, circle), 0) + lax.broadcasted_iota(
        jnp.int32, (circle, circle), 1)
    flip = jnp.where((place == 0) | (place == circle), 1.0, 0.0).astype(jnp.bfloat16)

    for copy in loads[:3]:
        copy.wait()
    profiles = kern[...].reshape(slots * basis * rows, circle).astype(jnp.bfloat16)
    taps[...] = jnp.dot(profiles, flip, preferred_element_type=jnp.float32)

    def build_row(i, carry):
        shift = starts[i] - (lat * rows + i - REACH)
        count = counts[i]
        for w in range(WINDOW):
            slot = w - shift
            live = jnp.where((slot >= 0) & (slot < count), 1.0, 0.0)
            slot = jnp.clip(slot, 0, slots - 1)
            for k in range(basis):
                line = taps[pl.ds((slot * basis + k) * rows + i, 1), :] * live
                turned = pltpu.roll(jnp.broadcast_to(line, (LANES, circle)), 0, 1, stride=1, stride_axis=0)
                base[i, pl.ds(k * LANES, LANES), pl.ds(w * circle, circle)] = turned.astype(jnp.bfloat16)
        return carry

    lax.fori_loop(0, rows, build_row, 0)

    take(theta_buf.at[pl.ds(0, L - 1)], th_sem.at[1])
    loads[8].wait()
    scale = jnp.concatenate([theta_buf[owner] for owner in range(L)], axis=1)

    def window(wide, e, i, h):
        cut = h * LANES
        pieces = []
        for w in range(WINDOW):
            pieces.append(wide[e, i + w, pl.ds(cut, circle - cut), :])
            if cut:
                pieces.append(wide[e, i + w, pl.ds(0, cut), :])
        return jnp.concatenate(pieces, axis=0)

    def mixed(prod, scale):
        total = prod[:LANES] * scale[0:1, :]
        for k in range(1, basis):
            total = total + prod[k * LANES:(k + 1) * LANES] * scale[k:k + 1, :]
        return total.astype(jnp.bfloat16)

    latest = jnp.where(lon < L // 2, L // 2, L // 2 - 1)

    def place_of(source, target):
        return lax.rem(source + L - (L // 2 if target < L // 2 else L // 2 - 1), L)

    def head_row(slot, carry):
        i = lax.rem(slot + REACH, rows)
        for e in range(members):
            both = jnp.concatenate([window(wide_a, e, i, h) for h in range(blocks)], axis=1)
            prod = jnp.dot(base[i], both, preferred_element_type=jnp.float32)
            for h in range(blocks):
                staged_a[e, slot, pl.ds(h * LANES, LANES), :] = mixed(
                    prod[:, h * head:(h + 1) * head], scale[:, :head])
            got_a[slot, lax.rem(lon + L - latest, L) * members + e] = staged_a[e, slot, lons(lon), :]
        return carry

    first = max(rows - REACH, 0)
    for step in range(1, L):
        incoming(0, step)
        for side in range(2):
            forward(side, 0, step, owners[step])
    mine[0].wait()
    arrived(0, 0)
    lax.fori_loop(0, first, head_row, 0)
    arrived(1, 0)
    lax.fori_loop(first, rows, head_row, 0)

    def back_head(target, e):
        return pltpu.make_async_remote_copy(
            src_ref=staged_a.at[e, :, lons(target), :], dst_ref=got_a.at[:, place_of(lon, target) * members + e],
            send_sem=back_send.at[0], recv_sem=a_recv.at[0],
            device_id={"lon": target}, device_id_type=MESH)

    outward = sorted(range(L), key=lambda p: min(p, L - 1 - p))
    for target in outward:
        @pl.when(lon != target)
        def _():
            for e in range(members):
                back_head(target, e).start()

    for step in range(1, L):
        incoming(1, step)
        forward(0, 1, step, owners[step])
    for step in range(1, L):
        for c in range(2, len(parts)):
            incoming(c, step)
        forward(1, 1, step, owners[step])
    mine[1].wait()
    arrived(0, 1)

    def back(slot, target, e, late):
        return pltpu.make_async_remote_copy(
            src_ref=staged_b.at[e, slot, lons(target), :], dst_ref=got_b.at[slot, place_of(lon, target) * members + e],
            send_sem=back_send.at[0], recv_sem=b_recv.at[slot, 0 if late else 1],
            device_id={"lon": target}, device_id_type=MESH)

    def send_one(slot, target):
        last = L // 2 if target < L // 2 else L // 2 - 1
        for late in (False, True):
            @pl.when((lon == last) if late else (lon != target) & (lon != last))
            def _():
                for e in range(members):
                    back(slot, target, e, late).start()

    lag = [min(BEHIND, rows) if 0 < target < L // 2 else 0 for target in range(L)]

    def send_part(slot, h):
        for target in outward:
            if (target * cols + cols - 1) // LANES == h:
                if lag[target]:
                    @pl.when(slot >= lag[target])
                    def _():
                        send_one(slot - lag[target], target)
                else:
                    send_one(slot, target)

    def conv_row(slot, carry):
        i = lax.rem(slot + REACH, rows)
        for e in range(members):
            for h in range(blocks):
                prod = jnp.dot(base[i], window(wide_b, e, i, h), preferred_element_type=jnp.float32)
                staged_b[e, slot, pl.ds(h * LANES, LANES), :] = mixed(prod, scale[:, head:])
                if e == members - 1 and h > 0:
                    send_part(slot, h - 1)
                if e == 0 and h == 0:
                    @pl.when(slot > 0)
                    def _():
                        send_part(slot - 1, blocks - 1)
            got_b[slot, lax.rem(lon + L - latest, L) * members + e] = staged_b[e, slot, lons(lon), :]
        return carry

    lax.fori_loop(0, first, conv_row, 0)
    arrived(1, 1)
    lax.fori_loop(first, rows, conv_row, 0)
    for copy in loads[3:8]:
        copy.wait()
    take(got_a.at[:, pl.ds(0, (L - 1) * members)], a_recv.at[0])

    def mlp_part(slot, low, high):
        i = lax.rem(slot + REACH, rows)
        fresh = (high - low - min(low, 1)) * members
        take(got_b.at[slot, pl.ds(0, fresh)], b_recv.at[slot, min(low, 1)])
        count = (high - low) * members
        here = pl.ds(low * members, count)
        values = jnp.concatenate(
            [got_a[slot, here].reshape(count * cols, head), got_b[slot, here].reshape(count * cols, chans - head)], axis=1)
        values = values.astype(jnp.float32)
        mean = jnp.mean(values, axis=-1, keepdims=True)
        diff = values - mean
        var = jnp.mean(diff * diff, axis=-1, keepdims=True)
        normed = (diff * lax.rsqrt(var + 1e-05) * gain[...][None, :]).astype(jnp.bfloat16)
        hidden = jnp.dot(normed, w_in[...], preferred_element_type=jnp.float32) + b_in[...][None, :]
        hidden = (0.5 * hidden * (1.0 + lax.erf(hidden * math.sqrt(0.5)))).astype(jnp.bfloat16)
        branch = jnp.dot(hidden, w_out[...], preferred_element_type=jnp.float32).reshape(high - low, members, cols, chans)
        for g in range(low, high):
            owned = pl.ds(lax.rem(latest + g, L) * members, members)
            out[owned, i] = (held[owned, i].astype(jnp.float32) + branch[g - low]).astype(jnp.bfloat16)

    def early_row(slot, carry):
        mlp_part(slot, 1, L)

        @pl.when(slot == 0)
        def _():
            send_part(rows - 1, blocks - 1)
            for target in range(L):
                for behind in range(lag[target], 0, -1):
                    send_one(rows - behind, target)

        return carry

    def late_row(slot, carry):
        mlp_part(slot, 0, 1)
        return carry

    lax.fori_loop(0, rows, early_row, 0)
    take(held.at[pl.ds(0, (L - 1) * members)], send_sem.at[0])
    take(theta_buf.at[pl.ds(0, L - 1)], th_sem.at[0])
    for side in range(2):
        @pl.when((has_down, has_up)[side])
        def _():
            for part in range(2):
                take(parts[part][0].at[:, pl.ds(0, REACH)], halo_send.at[side, part])
    lax.fori_loop(0, rows, late_row, 0)
    take(held.at[pl.ds(0, (L - 1) * members)], back_send.at[0])


def block(fields, theta, kern, starts, counts, gain, w_in, b_in, w_out, L, T):
    ens, rows, cols, chans = fields.shape
    members, circle = ens // L, cols * L
    basis = theta.shape[0]
    head = LANES
    tail = chans - head
    dma = pltpu.SemaphoreType.DMA
    bf16 = jnp.bfloat16
    return pl.pallas_call(
        functools.partial(block_kernel, L, T, members),
        out_shape=pltpu.VMEM(fields.shape, bf16),
        in_specs=[pl.BlockSpec(memory_space=pltpu.HBM)] * 9,
        out_specs=pl.BlockSpec(memory_space=pltpu.VMEM),
        scratch_shapes=[
            pltpu.VMEM((members, rows + 2 * REACH, circle, head), bf16),
            pltpu.VMEM((members, rows + 2 * REACH, circle, tail), bf16),
            pltpu.VMEM((rows, basis * LANES, WINDOW * circle), bf16),
            pltpu.VMEM((kern.shape[0] * basis * rows, circle), jnp.float32),
            pltpu.VMEM(kern.shape, jnp.float32),
            pltpu.SMEM(starts.shape, jnp.int32),
            pltpu.SMEM(counts.shape, jnp.int32),
            pltpu.VMEM(gain.shape, jnp.float32),
            pltpu.VMEM(w_in.shape, bf16),
            pltpu.VMEM(b_in.shape, jnp.float32),
            pltpu.VMEM(w_out.shape, bf16),
            pltpu.VMEM((L,) + theta.shape, jnp.float32),
            pltpu.VMEM((members, rows, circle, head), bf16),
            pltpu.VMEM((members, rows, circle, tail), bf16),
            pltpu.VMEM((rows, ens, cols, head), bf16),
            pltpu.VMEM((rows, ens, cols, tail), bf16),
            pltpu.VMEM(fields.shape, bf16),
            pltpu.SemaphoreType.REGULAR((2,)), pltpu.SemaphoreType.REGULAR((2,)), dma((1,)), dma((3, L - 1)), dma((2, 2)), dma((2, 2)), dma((2,)), dma((11,)), dma((1,)), dma((1,)), dma((rows, 2)),
        ],
        compiler_params=pltpu.CompilerParams(
            collective_id=0, has_side_effects=True, vmem_limit_bytes=52 * 2**20),
        name="block",
    )(fields, theta, kern, starts, counts, gain, w_in, b_in, w_out)


def with_halo(value, sides, width):
    for axis, dim in sides:
        size, length = (lax.axis_size(axis), value.shape[dim])
        up = [(i, (i + 1) % size) for i in range(size - 1)]
        down = [(j, i) for i, j in up]
        last = lax.slice_in_dim(value, length - width, length, axis=dim)
        initial = lax.slice_in_dim(value, 0, width, axis=dim)
        before = lax.ppermute(last, axis, up)
        after = lax.ppermute(initial, axis, down)
        value = jnp.concatenate([before, value, after], axis=dim)
    return value


def circle_tables(length):
    bins = length // 2 + 1
    points = jnp.arange(length, dtype=jnp.int32)
    freqs = jnp.arange(bins, dtype=jnp.int32)
    phase = points[:, None] * freqs[None, :] % length
    angle = phase.astype(jnp.float32) * (2.0 * math.pi / length)
    cosine = jnp.cos(angle)
    sine = jnp.sin(angle)
    onward = jnp.concatenate([cosine, -sine], axis=1)
    weight = jnp.where((freqs == 0) | (freqs == length // 2), 1.0, 2.0).astype(jnp.float32)
    backward = (
        jnp.concatenate([(cosine * weight[None, :]).T, (-sine * weight[None, :]).T], axis=0)
        / length
    )
    return (onward, backward, bins)


def forward(field, onward, bins):
    upper = onward.astype(jnp.bfloat16)
    lower = (onward - upper.astype(jnp.float32)).astype(jnp.bfloat16)
    spectrum = jnp.einsum("ejlc,lg->ejgc", field, upper, preferred_element_type=jnp.float32)
    spectrum = spectrum + jnp.einsum(
        "ejlc,lg->ejgc", field, lower, preferred_element_type=jnp.float32
    )
    return (spectrum[:, :, :bins], spectrum[:, :, bins:])


def mix_basis(kern_part, theta):
    mixed = kern_part[:, :, 0, :, None] * theta[0][None, None, None, :]
    for basis in range(1, kern_part.shape[2]):
        mixed = mixed + kern_part[:, :, basis, :, None] * theta[basis][None, None, None, :]
    return mixed


def spectral_shards(fields, kernel, theta, row_start, row_count, norm_gain, w_in, b_in, w_out):
    local = lax.all_to_all(fields, "lon", split_axis=3, concat_axis=2, tiled=True)
    members, band, circle, chans = local.shape
    onward, backward, bins = circle_tables(circle)
    widened = with_halo(local, (("lat", 1),), REACH)
    spec_re, spec_im = forward(widened, onward, bins)
    kern_all = jnp.einsum("irkm,mg->irkg", kernel, onward, precision=lax.Precision.HIGHEST)
    mixed_re = mix_basis(kern_all[..., :bins], theta)
    mixed_im = mix_basis(kern_all[..., bins:], theta)
    first_row = lax.axis_index("lat") * band - REACH
    span_rows = band + 2 * REACH
    slot_ids = jnp.arange(WINDOW, dtype=jnp.int32)
    offsets = row_start - first_row
    live_slot = slot_ids[None, :] < row_count[:, None]
    total_re = jnp.zeros((members, band, bins, chans), jnp.float32)
    total_im = jnp.zeros((members, band, bins, chans), jnp.float32)
    for span in range(span_rows):
        select = (live_slot & (offsets[:, None] + slot_ids[None, :] == span)).astype(jnp.float32)
        coef_re = jnp.einsum("is,isfc->ifc", select, mixed_re, precision=lax.Precision.HIGHEST)
        coef_im = jnp.einsum("is,isfc->ifc", select, mixed_im, precision=lax.Precision.HIGHEST)
        row_re = spec_re[:, span][:, None]
        row_im = spec_im[:, span][:, None]
        total_re = total_re + coef_re * row_re - coef_im * row_im
        total_im = total_im + coef_re * row_im + coef_im * row_re
    joined = jnp.concatenate([total_re, total_im], axis=2)
    conv = jnp.einsum("eigc,gl->eilc", joined, backward, precision=lax.Precision.HIGHEST).astype(
        jnp.bfloat16
    )
    values = lax.all_to_all(conv, "lon", split_axis=2, concat_axis=3, tiled=True).astype(
        jnp.float32
    )
    mean = jnp.mean(values, axis=-1, keepdims=True)
    var = jnp.mean((values - mean) ** 2, axis=-1, keepdims=True)
    normed = ((values - mean) * lax.rsqrt(var + 1e-05) * norm_gain).astype(jnp.bfloat16)
    hidden = jax.nn.gelu(
        jnp.einsum("eblc,ch->eblh", normed, w_in, preferred_element_type=jnp.float32) + b_in,
        approximate=False,
    ).astype(jnp.bfloat16)
    branch = jnp.einsum("eblh,hc->eblc", hidden, w_out, preferred_element_type=jnp.float32)
    return (fields.astype(jnp.float32) + branch).astype(jnp.bfloat16)


def shards(L, T, fields, kernel, theta, row_start, row_count, norm_gain, w_in, b_in, w_out):
    if fields.shape[0] % L:
        return spectral_shards(
            fields, kernel, theta, row_start, row_count, norm_gain, w_in, b_in, w_out
        )
    kern = jnp.transpose(kernel, (1, 2, 0, 3))
    return block(fields, theta, kern, row_start, row_count, norm_gain, w_in, b_in, w_out, L, T)


def solution(mesh):
    placed = (
        P(None, "lat", "lon", None),
        P("lat", None, None, None),
        P(None, "lon"),
        P("lat"),
        P("lat"),
        P(),
        P(),
        P(),
        P(),
    )
    return jax.shard_map(
        functools.partial(shards, mesh.shape["lon"], mesh.shape["lat"]),
        mesh=mesh, in_specs=placed, out_specs=P(None, "lat", "lon", None), check_vma=False,
    )
```

```python
import functools
import math

import jax
import jax.numpy as jnp
from jax import lax
from jax.experimental import pallas as pl
from jax.experimental.pallas import tpu as pltpu
from jax.sharding import PartitionSpec as P

REACH = 4
WINDOW = 2 * REACH + 1
LANES = 128
BEHIND = 2
MESH = pl.DeviceIdType.MESH


def channel_mlp(first, rest, gain, w_in, b_in, w_out):
    values = jnp.concatenate([first, rest], axis=1).astype(jnp.float32)
    mean = jnp.mean(values, axis=-1, keepdims=True)
    diff = values - mean
    var = jnp.mean(diff * diff, axis=-1, keepdims=True)
    normed = (diff * lax.rsqrt(var + 1e-05) * gain[...][None, :]).astype(jnp.bfloat16)
    hidden = jnp.dot(normed, w_in[...], preferred_element_type=jnp.float32) + b_in[...][None, :]
    hidden = (0.5 * hidden * (1.0 + lax.erf(hidden * math.sqrt(0.5)))).astype(jnp.bfloat16)
    return jnp.dot(hidden, w_out[...], preferred_element_type=jnp.float32)


def last_kernel(L, done, last_a, last_b, last_h, gain, w_in, b_in, w_out, out, piece, sem):
    lon = lax.axis_index("lon")
    ens, rows, cols, chans = out.shape
    members, _, head = last_a.shape
    latest = jnp.where(lon < L // 2, L // 2, L // 2 - 1)
    final = (rows - 1 + REACH) % rows
    others = [i for i in range(rows) if i != final]
    early, later = others[:5], others[5:]
    for i in early:
        pltpu.make_async_copy(done.at[:, i], out.at[:, i], sem.at[0]).start()
    branch = channel_mlp(
        last_a[...].reshape(members * cols, head), last_b[...].reshape(members * cols, chans - head),
        gain, w_in, b_in, w_out).reshape(members, cols, chans)
    piece[...] = (last_h[...].astype(jnp.float32) + branch).astype(jnp.bfloat16)
    copy = pltpu.make_async_copy(piece, out.at[pl.ds(latest * members, members), final], sem.at[1])
    copy.start()
    for i in later:
        pltpu.make_async_copy(done.at[:, i], out.at[:, i], sem.at[0]).start()
    for g in range(1, L):
        owned = pl.ds(lax.rem(latest + g, L) * members, members)
        pltpu.make_async_copy(done.at[owned, final], out.at[owned, final], sem.at[2]).start()
    if rows > 1:
        pltpu.make_async_copy(done.at[:, :rows - 1], out.at[:, :rows - 1], sem.at[0]).wait()
    pltpu.make_async_copy(done.at[:ens - members, 0], out.at[:ens - members, 0], sem.at[2]).wait()
    copy.wait()


def block_kernel(
    L, T, members, fields, theta, kern_hbm, starts_hbm, counts_hbm, gain_hbm, w_in_hbm, b_in_hbm, w_out_hbm,
    out, last_a, last_b, last_h, gain, w_in, b_in, w_out,
    wide_a, wide_b, base, taps, kern, starts, counts, theta_buf,
    staged_a, staged_b, got_a, got_b, held,
    far_sem, lat_sem, send_sem, recv_sem, halo_send, halo_recv, th_sem, local_sem, back_send, a_recv, b_recv,
):
    lat, lon = lax.axis_index("lat"), lax.axis_index("lon")
    up, down = lax.rem(lat + 1, T), lax.rem(lat + T - 1, T)
    has_up, has_down = lat < T - 1, lat > 0
    ens, rows, cols, chans = held.shape
    circle = wide_a.shape[2]
    slots, basis = kern.shape[:2]
    head = wide_a.shape[3]
    blocks = circle // LANES

    pairs = ((kern_hbm, kern), (starts_hbm, starts), (counts_hbm, counts), (gain_hbm, gain),
             (w_in_hbm, w_in), (b_in_hbm, b_in), (w_out_hbm, w_out), (fields, held), (theta, theta_buf.at[lon]))
    loads = [pltpu.make_async_copy(a, b, local_sem.at[n]) for n, (a, b) in enumerate(pairs)]
    barrier = pltpu.get_barrier_semaphore()
    half = L // 2
    low = lon < half
    inward, outward_by = jnp.where(low, lon + 1, lon - 1), jnp.where(low, lon - 1, lon + 1)
    middle = (lon == half - 1) | (lon == half)
    at_end = (lon == 0) | (lon == L - 1)
    relayed = ((lon == 1) | (lon == L - 2)) if L > 3 else lon < 0
    beside = ((down, has_down), (up, has_up))

    def signal(sem, when, **device):
        @pl.when(when)
        def _():
            pl.semaphore_signal(sem, inc=1, device_id=device, device_id_type=MESH)

    signal(barrier, ~at_end, lon=outward_by)
    signal(barrier, middle, lon=inward)
    for other, there in beside:
        signal(barrier, there & ~relayed, lat=other)
    greeted = [jnp.where(there & ~relayed, 1, 0) for _, there in beside]
    pl.semaphore_wait(barrier, 1 + greeted[0] + greeted[1])

    def learn(side, when):
        @pl.when(when)
        def _():
            pl.semaphore_wait(far_sem.at[side], 1)

    def take(ref, sem):
        pltpu.make_async_copy(ref, ref, sem).wait()

    owners = [lax.rem(lon + L - step, L) for step in range(L)]

    def lons(owner):
        return pl.ds(pl.multiple_of(owner * cols, cols), cols)

    def member(owner):
        return pl.ds(owner * members, members)

    parts = [(wide_a, pl.ds(0, head), 0, rows), (wide_b, pl.ds(head, chans - head), 0, REACH)]
    if rows > REACH:
        parts.append((wide_b, pl.ds(head, chans - head), REACH, rows - REACH))
    def send_theta(peer):
        pltpu.make_async_remote_copy(
            src_ref=theta, dst_ref=theta_buf.at[lon], send_sem=th_sem.at[0], recv_sem=th_sem.at[1],
            device_id={"lon": peer}, device_id_type=MESH).start()

    def outgoing(c, peer):
        wide, chan, low, size = parts[c]
        return pltpu.make_async_remote_copy(
            src_ref=fields.at[member(peer), pl.ds(low, size), :, chan],
            dst_ref=wide.at[:, pl.ds(REACH + low, size), lons(lon), :],
            send_sem=send_sem.at[0], recv_sem=recv_sem.at[c, lax.rem(peer - lon + L, L) - 1],
            device_id={"lon": peer}, device_id_type=MESH)

    def incoming(c, step):
        wide, chan, low, size = parts[c]
        take(wide.at[:, pl.ds(REACH + low, size), lons(owners[step]), :], recv_sem.at[c, step - 1])

    def both_ways(distance, act):
        for peer, known in ((lon - distance, lon >= distance), (lon + distance, lon + distance < L)):
            pl.when(known)(functools.partial(act, peer))

    def begin(peer):
        outgoing(0, peer).start()
        send_theta(peer)

    begin(inward)
    signal(far_sem.at[1], ~middle, lon=inward)
    for copy in loads[:3]:
        copy.start()
    for side, (other, there) in enumerate(beside):
        signal(lat_sem.at[1 - side], there & at_end & (L > 3), lat=other)
    inner_count = jnp.where(low, L - 1 - lon, lon)
    outer_count = L - 1 - inner_count
    for distance in range(1, L):
        known = distance <= outer_count
        learn(1, known)
        signal(far_sem.at[1], known & ~middle, lon=inward)
        if distance == 1:
            signal(far_sem.at[0], known, lon=outward_by)
            signal(far_sem.at[0], known & middle, lon=inward)
        else:
            signal(far_sem.at[0], known & middle, lon=inward)
        pl.when(known)(functools.partial(begin, jnp.where(low, lon - distance, lon + distance)))
        if distance > 1:
            known = distance <= inner_count
            learn(0, known)
            signal(far_sem.at[0], known & ~at_end, lon=outward_by)
            pl.when(known)(functools.partial(begin, jnp.where(low, lon + distance, lon - distance)))
    for side, (other, there) in enumerate(beside):
        @pl.when(there & (at_end | relayed) & (L > 3))
        def _():
            pl.semaphore_wait(lat_sem.at[side], 1)

        signal(lat_sem.at[side], there & at_end & (L > 3), lon=inward)
    for c in range(1, len(parts)):
        for distance in range(1, L):
            both_ways(distance, lambda peer: outgoing(c, peer).start())
    mine = [
        pltpu.make_async_copy(
            fields.at[member(lon), :, :, chan], wide.at[:, pl.ds(REACH, rows), lons(lon), :], local_sem.at[len(pairs)])
        for wide, chan, _, _ in parts[:2]]
    for copy in mine + loads[3:]:
        copy.start()

    def forward(side, part, step, owner):
        wide, chan = parts[part][:2]
        source, target, other, there = ((0, REACH + rows, down, has_down), (rows - REACH, 0, up, has_up))[side]
        if step:
            src = wide.at[:, pl.ds(REACH + source, REACH), lons(owner), :]
        else:
            src = fields.at[member(owner), pl.ds(source, REACH), :, chan]
        copy = pltpu.make_async_remote_copy(
            src_ref=src, dst_ref=wide.at[:, pl.ds(target, REACH), lons(owner), :],
            send_sem=halo_send.at[side], recv_sem=halo_recv.at[side, part],
            device_id={"lat": other}, device_id_type=MESH)
        pl.when(there)(copy.start)

    def arrived(side, part):
        @pl.when((has_up, has_down)[side])
        def _():
            target = (REACH + rows, 0)[side]
            take(parts[part][0].at[:, pl.ds(target, REACH)], halo_recv.at[side, part])

    for side in range(2):
        for part in range(2):
            forward(side, part, 0, lon)

    @pl.when(lat == 0)
    def _():
        for wide in (wide_a, wide_b):
            wide[:, :REACH] = jnp.zeros_like(wide[:, :REACH])

    @pl.when(lat == T - 1)
    def _():
        for wide in (wide_a, wide_b):
            wide[:, REACH + rows:] = jnp.zeros_like(wide[:, REACH + rows:])

    place = lax.broadcasted_iota(jnp.int32, (circle, circle), 0) + lax.broadcasted_iota(
        jnp.int32, (circle, circle), 1)
    flip = jnp.where((place == 0) | (place == circle), 1.0, 0.0).astype(jnp.bfloat16)

    for copy in loads[:3]:
        copy.wait()
    profiles = kern[...].reshape(slots * basis * rows, circle).astype(jnp.bfloat16)
    taps[...] = jnp.dot(profiles, flip, preferred_element_type=jnp.float32)

    def build_row(i, carry):
        shift = starts[i] - (lat * rows + i - REACH)
        count = counts[i]
        for w in range(WINDOW):
            slot = w - shift
            live = jnp.where((slot >= 0) & (slot < count), 1.0, 0.0)
            slot = jnp.clip(slot, 0, slots - 1)
            for k in range(basis):
                line = taps[pl.ds((slot * basis + k) * rows + i, 1), :] * live
                turned = pltpu.roll(jnp.broadcast_to(line, (LANES, circle)), 0, 1, stride=1, stride_axis=0)
                base[i, pl.ds(k * LANES, LANES), pl.ds(w * circle, circle)] = turned.astype(jnp.bfloat16)
        return carry

    lax.fori_loop(0, rows, build_row, 0)

    take(theta_buf.at[pl.ds(0, L - 1)], th_sem.at[1])
    loads[8].wait()
    scale = jnp.concatenate([theta_buf[owner] for owner in range(L)], axis=1)

    def window(wide, e, i, h):
        cut = h * LANES
        pieces = []
        for w in range(WINDOW):
            pieces.append(wide[e, i + w, pl.ds(cut, circle - cut), :])
            if cut:
                pieces.append(wide[e, i + w, pl.ds(0, cut), :])
        return jnp.concatenate(pieces, axis=0)

    def mixed(prod, scale):
        total = prod[:LANES] * scale[0:1, :]
        for k in range(1, basis):
            total = total + prod[k * LANES:(k + 1) * LANES] * scale[k:k + 1, :]
        return total.astype(jnp.bfloat16)

    latest = jnp.where(lon < L // 2, L // 2, L // 2 - 1)

    def place_of(source, target):
        return lax.rem(source + L - (L // 2 if target < L // 2 else L // 2 - 1), L)

    def head_row(slot, carry):
        i = lax.rem(slot + REACH, rows)
        for e in range(members):
            both = jnp.concatenate([window(wide_a, e, i, h) for h in range(blocks)], axis=1)
            prod = jnp.dot(base[i], both, preferred_element_type=jnp.float32)
            for h in range(blocks):
                staged_a[e, slot, pl.ds(h * LANES, LANES), :] = mixed(
                    prod[:, h * head:(h + 1) * head], scale[:, :head])
            got_a[slot, lax.rem(lon + L - latest, L) * members + e] = staged_a[e, slot, lons(lon), :]
        return carry

    first = max(rows - REACH, 0)
    for step in range(1, L):
        incoming(0, step)
        for side in range(2):
            forward(side, 0, step, owners[step])
    take(held.at[member(0)], local_sem.at[len(pairs)])
    arrived(0, 0)
    lax.fori_loop(0, first, head_row, 0)
    arrived(1, 0)
    lax.fori_loop(first, rows, head_row, 0)

    def back_head(target, e):
        return pltpu.make_async_remote_copy(
            src_ref=staged_a.at[e, :, lons(target), :], dst_ref=got_a.at[:, place_of(lon, target) * members + e],
            send_sem=back_send.at[0], recv_sem=a_recv.at[0],
            device_id={"lon": target}, device_id_type=MESH)

    outward = sorted(range(L), key=lambda p: min(p, L - 1 - p))
    for target in outward:
        @pl.when(lon != target)
        def _():
            for e in range(members):
                back_head(target, e).start()

    for step in range(1, L):
        incoming(1, step)
        forward(0, 1, step, owners[step])
    for step in range(1, L):
        for c in range(2, len(parts)):
            incoming(c, step)
        forward(1, 1, step, owners[step])
    arrived(0, 1)

    def back(slot, target, e, late):
        return pltpu.make_async_remote_copy(
            src_ref=staged_b.at[e, slot, lons(target), :], dst_ref=got_b.at[slot, place_of(lon, target) * members + e],
            send_sem=back_send.at[0], recv_sem=b_recv.at[slot, 0 if late else 1],
            device_id={"lon": target}, device_id_type=MESH)

    def send_one(slot, target):
        last = L // 2 if target < L // 2 else L // 2 - 1
        for late in (False, True):
            @pl.when((lon == last) if late else (lon != target) & (lon != last))
            def _():
                for e in range(members):
                    back(slot, target, e, late).start()

    lag = [min(BEHIND, rows) if 0 < target < L // 2 else 0 for target in range(L)]

    def send_part(slot, h):
        for target in outward:
            if (target * cols + cols - 1) // LANES == h:
                if lag[target]:
                    @pl.when(slot >= lag[target])
                    def _():
                        send_one(slot - lag[target], target)
                else:
                    send_one(slot, target)

    def conv_row(slot, carry):
        i = lax.rem(slot + REACH, rows)
        for e in range(members):
            for h in range(blocks):
                prod = jnp.dot(base[i], window(wide_b, e, i, h), preferred_element_type=jnp.float32)
                staged_b[e, slot, pl.ds(h * LANES, LANES), :] = mixed(prod, scale[:, head:])
                if e == members - 1 and h > 0:
                    send_part(slot, h - 1)
                if e == 0 and h == 0:
                    @pl.when(slot > 0)
                    def _():
                        send_part(slot - 1, blocks - 1)
            got_b[slot, lax.rem(lon + L - latest, L) * members + e] = staged_b[e, slot, lons(lon), :]
        return carry

    lax.fori_loop(0, first, conv_row, 0)
    arrived(1, 1)
    lax.fori_loop(first, rows, conv_row, 0)
    for copy in loads[3:8]:
        copy.wait()
    take(got_a.at[:, pl.ds(0, (L - 1) * members)], a_recv.at[0])

    def mlp_part(slot, low, high):
        i = lax.rem(slot + REACH, rows)
        fresh = (high - low - min(low, 1)) * members
        take(got_b.at[slot, pl.ds(0, fresh)], b_recv.at[slot, min(low, 1)])
        count = (high - low) * members
        here = pl.ds(low * members, count)
        branch = channel_mlp(
            got_a[slot, here].reshape(count * cols, head), got_b[slot, here].reshape(count * cols, chans - head),
            gain, w_in, b_in, w_out).reshape(high - low, members, cols, chans)
        for g in range(low, high):
            owned = pl.ds(lax.rem(latest + g, L) * members, members)
            out[owned, i] = (held[owned, i].astype(jnp.float32) + branch[g - low]).astype(jnp.bfloat16)

    def early_row(slot, carry):
        mlp_part(slot, 1, L)

        @pl.when(slot == 0)
        def _():
            send_part(rows - 1, blocks - 1)
            for target in range(L):
                for behind in range(lag[target], 0, -1):
                    send_one(rows - behind, target)

        return carry

    def late_row(slot, carry):
        mlp_part(slot, 0, 1)
        return carry

    lax.fori_loop(0, rows, early_row, 0)
    take(held.at[pl.ds(0, (L - 1) * members)], send_sem.at[0])
    take(theta_buf.at[pl.ds(0, L - 1)], th_sem.at[0])
    for side in range(2):
        @pl.when((has_down, has_up)[side])
        def _():
            take(held.at[:, pl.ds(0, REACH)], halo_send.at[side])
    lax.fori_loop(0, rows - 1, late_row, 0)
    final = (rows - 1 + REACH) % rows
    last_h[...] = held[pl.ds(latest * members, members), final]
    last_a[...] = got_a[rows - 1, pl.ds(0, members)]
    take(got_b.at[rows - 1, pl.ds(0, members)], b_recv.at[rows - 1, 0])
    last_b[...] = got_b[rows - 1, pl.ds(0, members)]
    take(held.at[pl.ds(0, (L - 1) * members)], back_send.at[0])


def block(fields, theta, kern, starts, counts, gain, w_in, b_in, w_out, L, T):
    ens, rows, cols, chans = fields.shape
    members, circle = ens // L, cols * L
    basis = theta.shape[0]
    head = LANES
    tail = chans - head
    dma = pltpu.SemaphoreType.DMA
    bf16 = jnp.bfloat16
    kept = (
        pltpu.VMEM(fields.shape, bf16), pltpu.VMEM((members, cols, head), bf16), pltpu.VMEM((members, cols, tail), bf16),
        pltpu.VMEM((members, cols, chans), bf16), pltpu.VMEM(gain.shape, jnp.float32), pltpu.VMEM(w_in.shape, bf16),
        pltpu.VMEM(b_in.shape, jnp.float32), pltpu.VMEM(w_out.shape, bf16))
    in_vmem = pl.BlockSpec(memory_space=pltpu.VMEM)
    parts = pl.pallas_call(
        functools.partial(block_kernel, L, T, members),
        out_shape=kept,
        in_specs=[pl.BlockSpec(memory_space=pltpu.HBM)] * 9,
        out_specs=[in_vmem] * len(kept),
        scratch_shapes=[
            pltpu.VMEM((members, rows + 2 * REACH, circle, head), bf16),
            pltpu.VMEM((members, rows + 2 * REACH, circle, tail), bf16),
            pltpu.VMEM((rows, basis * LANES, WINDOW * circle), bf16),
            pltpu.VMEM((kern.shape[0] * basis * rows, circle), jnp.float32),
            pltpu.VMEM(kern.shape, jnp.float32),
            pltpu.SMEM(starts.shape, jnp.int32),
            pltpu.SMEM(counts.shape, jnp.int32),
            pltpu.VMEM((L,) + theta.shape, jnp.float32),
            pltpu.VMEM((members, rows, circle, head), bf16),
            pltpu.VMEM((members, rows, circle, tail), bf16),
            pltpu.VMEM((rows, ens, cols, head), bf16),
            pltpu.VMEM((rows, ens, cols, tail), bf16),
            pltpu.VMEM(fields.shape, bf16),
            pltpu.SemaphoreType.REGULAR((2,)), pltpu.SemaphoreType.REGULAR((2,)), dma((1,)), dma((3, L - 1)), dma((2,)), dma((2, 2)), dma((2,)), dma((10,)), dma((1,)), dma((1,)), dma((rows, 2)),
        ],
        compiler_params=pltpu.CompilerParams(
            collective_id=0, has_side_effects=True, vmem_limit_bytes=48 * 2**20),
        name="block",
    )(*(pltpu.with_memory_space_constraint(v, pltpu.HBM)
        for v in (fields, theta, kern, starts, counts, gain, w_in, b_in, w_out)))
    return pl.pallas_call(
        functools.partial(last_kernel, L),
        out_shape=jax.ShapeDtypeStruct(fields.shape, bf16),
        in_specs=[in_vmem] * len(kept),
        out_specs=pl.BlockSpec(memory_space=pltpu.HBM),
        scratch_shapes=[pltpu.VMEM((members, cols, chans), bf16), dma((3,))],
        compiler_params=pltpu.CompilerParams(vmem_limit_bytes=8 * 2**20),
        name="last",
    )(*parts)


def with_halo(value, sides, width):
    for axis, dim in sides:
        size, length = (lax.axis_size(axis), value.shape[dim])
        up = [(i, (i + 1) % size) for i in range(size - 1)]
        down = [(j, i) for i, j in up]
        last = lax.slice_in_dim(value, length - width, length, axis=dim)
        initial = lax.slice_in_dim(value, 0, width, axis=dim)
        before = lax.ppermute(last, axis, up)
        after = lax.ppermute(initial, axis, down)
        value = jnp.concatenate([before, value, after], axis=dim)
    return value


def circle_tables(length):
    bins = length // 2 + 1
    points = jnp.arange(length, dtype=jnp.int32)
    freqs = jnp.arange(bins, dtype=jnp.int32)
    phase = points[:, None] * freqs[None, :] % length
    angle = phase.astype(jnp.float32) * (2.0 * math.pi / length)
    cosine = jnp.cos(angle)
    sine = jnp.sin(angle)
    onward = jnp.concatenate([cosine, -sine], axis=1)
    weight = jnp.where((freqs == 0) | (freqs == length // 2), 1.0, 2.0).astype(jnp.float32)
    backward = (
        jnp.concatenate([(cosine * weight[None, :]).T, (-sine * weight[None, :]).T], axis=0)
        / length
    )
    return (onward, backward, bins)


def forward(field, onward, bins):
    upper = onward.astype(jnp.bfloat16)
    lower = (onward - upper.astype(jnp.float32)).astype(jnp.bfloat16)
    spectrum = jnp.einsum("ejlc,lg->ejgc", field, upper, preferred_element_type=jnp.float32)
    spectrum = spectrum + jnp.einsum(
        "ejlc,lg->ejgc", field, lower, preferred_element_type=jnp.float32
    )
    return (spectrum[:, :, :bins], spectrum[:, :, bins:])


def mix_basis(kern_part, theta):
    mixed = kern_part[:, :, 0, :, None] * theta[0][None, None, None, :]
    for basis in range(1, kern_part.shape[2]):
        mixed = mixed + kern_part[:, :, basis, :, None] * theta[basis][None, None, None, :]
    return mixed


def spectral_shards(fields, kernel, theta, row_start, row_count, norm_gain, w_in, b_in, w_out):
    local = lax.all_to_all(fields, "lon", split_axis=3, concat_axis=2, tiled=True)
    members, band, circle, chans = local.shape
    onward, backward, bins = circle_tables(circle)
    widened = with_halo(local, (("lat", 1),), REACH)
    spec_re, spec_im = forward(widened, onward, bins)
    kern_all = jnp.einsum("irkm,mg->irkg", kernel, onward, precision=lax.Precision.HIGHEST)
    mixed_re = mix_basis(kern_all[..., :bins], theta)
    mixed_im = mix_basis(kern_all[..., bins:], theta)
    first_row = lax.axis_index("lat") * band - REACH
    span_rows = band + 2 * REACH
    slot_ids = jnp.arange(WINDOW, dtype=jnp.int32)
    offsets = row_start - first_row
    live_slot = slot_ids[None, :] < row_count[:, None]
    total_re = jnp.zeros((members, band, bins, chans), jnp.float32)
    total_im = jnp.zeros((members, band, bins, chans), jnp.float32)
    for span in range(span_rows):
        select = (live_slot & (offsets[:, None] + slot_ids[None, :] == span)).astype(jnp.float32)
        coef_re = jnp.einsum("is,isfc->ifc", select, mixed_re, precision=lax.Precision.HIGHEST)
        coef_im = jnp.einsum("is,isfc->ifc", select, mixed_im, precision=lax.Precision.HIGHEST)
        row_re = spec_re[:, span][:, None]
        row_im = spec_im[:, span][:, None]
        total_re = total_re + coef_re * row_re - coef_im * row_im
        total_im = total_im + coef_re * row_im + coef_im * row_re
    joined = jnp.concatenate([total_re, total_im], axis=2)
    conv = jnp.einsum("eigc,gl->eilc", joined, backward, precision=lax.Precision.HIGHEST).astype(
        jnp.bfloat16
    )
    values = lax.all_to_all(conv, "lon", split_axis=2, concat_axis=3, tiled=True).astype(
        jnp.float32
    )
    mean = jnp.mean(values, axis=-1, keepdims=True)
    var = jnp.mean((values - mean) ** 2, axis=-1, keepdims=True)
    normed = ((values - mean) * lax.rsqrt(var + 1e-05) * norm_gain).astype(jnp.bfloat16)
    hidden = jax.nn.gelu(
        jnp.einsum("eblc,ch->eblh", normed, w_in, preferred_element_type=jnp.float32) + b_in,
        approximate=False,
    ).astype(jnp.bfloat16)
    branch = jnp.einsum("eblh,hc->eblc", hidden, w_out, preferred_element_type=jnp.float32)
    return (fields.astype(jnp.float32) + branch).astype(jnp.bfloat16)


def shards(L, T, fields, kernel, theta, row_start, row_count, norm_gain, w_in, b_in, w_out):
    if L == 1 or fields.shape[0] % L:
        return spectral_shards(
            fields, kernel, theta, row_start, row_count, norm_gain, w_in, b_in, w_out
        )
    kern = jnp.transpose(kernel, (1, 2, 0, 3))
    return block(fields, theta, kern, row_start, row_count, norm_gain, w_in, b_in, w_out, L, T)


def solution(mesh):
    placed = (
        P(None, "lat", "lon", None),
        P("lat", None, None, None),
        P(None, "lon"),
        P("lat"),
        P("lat"),
        P(),
        P(),
        P(),
        P(),
    )
    return jax.shard_map(
        functools.partial(shards, mesh.shape["lon"], mesh.shape["lat"]),
        mesh=mesh, in_specs=placed, out_specs=P(None, "lat", "lon", None), check_vma=False,
    )
```

```python
import functools
import math

import jax
import jax.numpy as jnp
from jax import lax
from jax.experimental import pallas as pl
from jax.experimental.pallas import tpu as pltpu
from jax.sharding import PartitionSpec as P

REACH = 4
WINDOW = 2 * REACH + 1
LANES = 128
BEHIND = 2
MESH = pl.DeviceIdType.MESH


def channel_mlp(first, rest, gain, w_in, b_in, w_out):
    values = jnp.concatenate([first, rest], axis=1).astype(jnp.float32)
    mean = jnp.mean(values, axis=-1, keepdims=True)
    diff = values - mean
    var = jnp.mean(diff * diff, axis=-1, keepdims=True)
    normed = (diff * lax.rsqrt(var + 1e-05) * gain[...][None, :]).astype(jnp.bfloat16)
    hidden = jnp.dot(normed, w_in[...], preferred_element_type=jnp.float32) + b_in[...][None, :]
    hidden = (0.5 * hidden * (1.0 + lax.erf(hidden * math.sqrt(0.5)))).astype(jnp.bfloat16)
    return jnp.dot(hidden, w_out[...], preferred_element_type=jnp.float32)


def last_kernel(L, done, last_a, last_b, last_h, gain, w_in, b_in, w_out, out, piece, sem):
    lon = lax.axis_index("lon")
    ens, rows, cols, chans = out.shape
    members, _, head = last_a.shape
    latest = jnp.where(lon < L // 2, L // 2, L // 2 - 1)
    final = (rows - 1 + REACH) % rows
    for e in range(ens):
        pltpu.make_async_copy(done.at[e, final + 1:], out.at[e, final + 1:], sem.at[0]).start()
        if e < ens // 2:
            pltpu.make_async_copy(done.at[e, :final], out.at[e, :final], sem.at[0]).start()
    branch = channel_mlp(
        last_a[...].reshape(members * cols, head), last_b[...].reshape(members * cols, chans - head),
        gain, w_in, b_in, w_out).reshape(members, cols, chans)
    piece[...] = (last_h[...].astype(jnp.float32) + branch).astype(jnp.bfloat16)
    copy = pltpu.make_async_copy(piece, out.at[pl.ds(latest * members, members), final], sem.at[1])
    copy.start()
    for e in range(ens // 2, ens):
        pltpu.make_async_copy(done.at[e, :final], out.at[e, :final], sem.at[0]).start()
    for g in range(1, L):
        owned = pl.ds(lax.rem(latest + g, L) * members, members)
        pltpu.make_async_copy(done.at[owned, final], out.at[owned, final], sem.at[2]).start()
    if rows > 1:
        pltpu.make_async_copy(done.at[:, :rows - 1], out.at[:, :rows - 1], sem.at[0]).wait()
    pltpu.make_async_copy(done.at[:ens - members, 0], out.at[:ens - members, 0], sem.at[2]).wait()
    copy.wait()


def block_kernel(
    L, T, members, fields, theta, kern_hbm, starts_hbm, counts_hbm, gain_hbm, w_in_hbm, b_in_hbm, w_out_hbm,
    out, last_a, last_b, last_h, gain, w_in, b_in, w_out,
    wide_a, wide_b, base, taps, kern, starts, counts, theta_buf,
    staged_a, staged_b, got_a, got_b, held,
    far_sem, lat_sem, send_sem, recv_sem, halo_send, halo_recv, th_sem, local_sem, back_send, a_recv, b_recv,
):
    lat, lon = lax.axis_index("lat"), lax.axis_index("lon")
    up, down = lax.rem(lat + 1, T), lax.rem(lat + T - 1, T)
    has_up, has_down = lat < T - 1, lat > 0
    ens, rows, cols, chans = held.shape
    circle = wide_a.shape[2]
    slots, basis = kern.shape[:2]
    head = wide_a.shape[3]
    blocks = circle // LANES

    pairs = ((kern_hbm, kern), (starts_hbm, starts), (counts_hbm, counts), (gain_hbm, gain),
             (w_in_hbm, w_in), (b_in_hbm, b_in), (w_out_hbm, w_out), (fields, held), (theta, theta_buf.at[lon]))
    loads = [pltpu.make_async_copy(a, b, local_sem.at[n]) for n, (a, b) in enumerate(pairs)]
    barrier = pltpu.get_barrier_semaphore()
    half = L // 2
    low = lon < half
    inward, outward_by = jnp.where(low, lon + 1, lon - 1), jnp.where(low, lon - 1, lon + 1)
    middle = (lon == half - 1) | (lon == half)
    at_end = (lon == 0) | (lon == L - 1)
    relayed = ((lon == 1) | (lon == L - 2)) if L > 3 else lon < 0
    beside = ((down, has_down), (up, has_up))

    def signal(sem, when, **device):
        @pl.when(when)
        def _():
            pl.semaphore_signal(sem, inc=1, device_id=device, device_id_type=MESH)

    signal(barrier, ~at_end, lon=outward_by)
    signal(barrier, middle, lon=inward)
    for other, there in beside:
        signal(barrier, there & ~relayed, lat=other)
    greeted = [jnp.where(there & ~relayed, 1, 0) for _, there in beside]
    pl.semaphore_wait(barrier, 1 + greeted[0] + greeted[1])

    def learn(side, when):
        @pl.when(when)
        def _():
            pl.semaphore_wait(far_sem.at[side], 1)

    def take(ref, sem):
        pltpu.make_async_copy(ref, ref, sem).wait()

    owners = [lax.rem(lon + L - step, L) for step in range(L)]

    def lons(owner):
        return pl.ds(pl.multiple_of(owner * cols, cols), cols)

    def member(owner):
        return pl.ds(owner * members, members)

    parts = [(wide_a, pl.ds(0, head), 0, rows), (wide_b, pl.ds(head, chans - head), 0, REACH)]
    if rows > REACH:
        parts.append((wide_b, pl.ds(head, chans - head), REACH, rows - REACH))
    def send_theta(peer):
        pltpu.make_async_remote_copy(
            src_ref=theta, dst_ref=theta_buf.at[lon], send_sem=th_sem.at[0], recv_sem=th_sem.at[1],
            device_id={"lon": peer}, device_id_type=MESH).start()

    def outgoing(c, peer):
        wide, chan, low, size = parts[c]
        return pltpu.make_async_remote_copy(
            src_ref=fields.at[member(peer), pl.ds(low, size), :, chan],
            dst_ref=wide.at[:, pl.ds(REACH + low, size), lons(lon), :],
            send_sem=send_sem.at[0], recv_sem=recv_sem.at[c, lax.rem(peer - lon + L, L) - 1],
            device_id={"lon": peer}, device_id_type=MESH)

    def incoming(c, step):
        wide, chan, low, size = parts[c]
        take(wide.at[:, pl.ds(REACH + low, size), lons(owners[step]), :], recv_sem.at[c, step - 1])

    def both_ways(distance, act):
        for peer, known in ((lon - distance, lon >= distance), (lon + distance, lon + distance < L)):
            pl.when(known)(functools.partial(act, peer))

    def begin(peer):
        outgoing(0, peer).start()
        send_theta(peer)

    begin(inward)
    signal(far_sem.at[1], ~middle, lon=inward)
    for copy in loads[:3]:
        copy.start()
    for side, (other, there) in enumerate(beside):
        signal(lat_sem.at[1 - side], there & at_end & (L > 3), lat=other)
    inner_count = jnp.where(low, L - 1 - lon, lon)
    outer_count = L - 1 - inner_count
    for distance in range(1, L):
        known = distance <= outer_count
        learn(1, known)
        signal(far_sem.at[1], known & ~middle, lon=inward)
        if distance == 1:
            signal(far_sem.at[0], known, lon=outward_by)
            signal(far_sem.at[0], known & middle, lon=inward)
        else:
            signal(far_sem.at[0], known & middle, lon=inward)
        pl.when(known)(functools.partial(begin, jnp.where(low, lon - distance, lon + distance)))
        if distance > 1:
            known = distance <= inner_count
            learn(0, known)
            signal(far_sem.at[0], known & ~at_end, lon=outward_by)
            pl.when(known)(functools.partial(begin, jnp.where(low, lon + distance, lon - distance)))
    for side, (other, there) in enumerate(beside):
        @pl.when(there & (at_end | relayed) & (L > 3))
        def _():
            pl.semaphore_wait(lat_sem.at[side], 1)

        signal(lat_sem.at[side], there & at_end & (L > 3), lon=inward)
    for c in range(1, len(parts)):
        for distance in range(1, L):
            both_ways(distance, lambda peer: outgoing(c, peer).start())
    mine = [
        pltpu.make_async_copy(
            fields.at[member(lon), :, :, chan], wide.at[:, pl.ds(REACH, rows), lons(lon), :], local_sem.at[len(pairs)])
        for wide, chan, _, _ in parts[:2]]
    for copy in mine + loads[3:]:
        copy.start()

    def forward(side, part, step, owner):
        wide, chan = parts[part][:2]
        source, target, other, there = ((0, REACH + rows, down, has_down), (rows - REACH, 0, up, has_up))[side]
        if step:
            src = wide.at[:, pl.ds(REACH + source, REACH), lons(owner), :]
        else:
            src = fields.at[member(owner), pl.ds(source, REACH), :, chan]
        copy = pltpu.make_async_remote_copy(
            src_ref=src, dst_ref=wide.at[:, pl.ds(target, REACH), lons(owner), :],
            send_sem=halo_send.at[side], recv_sem=halo_recv.at[side, part],
            device_id={"lat": other}, device_id_type=MESH)
        pl.when(there)(copy.start)

    def arrived(side, part):
        @pl.when((has_up, has_down)[side])
        def _():
            target = (REACH + rows, 0)[side]
            take(parts[part][0].at[:, pl.ds(target, REACH)], halo_recv.at[side, part])

    for side in range(2):
        for part in range(2):
            forward(side, part, 0, lon)

    @pl.when(lat == 0)
    def _():
        for wide in (wide_a, wide_b):
            wide[:, :REACH] = jnp.zeros_like(wide[:, :REACH])

    @pl.when(lat == T - 1)
    def _():
        for wide in (wide_a, wide_b):
            wide[:, REACH + rows:] = jnp.zeros_like(wide[:, REACH + rows:])

    place = lax.broadcasted_iota(jnp.int32, (circle, circle), 0) + lax.broadcasted_iota(
        jnp.int32, (circle, circle), 1)
    flip = jnp.where((place == 0) | (place == circle), 1.0, 0.0).astype(jnp.bfloat16)

    for copy in loads[:3]:
        copy.wait()
    profiles = kern[...].reshape(slots * basis * rows, circle).astype(jnp.bfloat16)
    taps[...] = jnp.dot(profiles, flip, preferred_element_type=jnp.float32)

    def build_row(i, carry):
        shift = starts[i] - (lat * rows + i - REACH)
        count = counts[i]
        for w in range(WINDOW):
            slot = w - shift
            live = jnp.where((slot >= 0) & (slot < count), 1.0, 0.0)
            slot = jnp.clip(slot, 0, slots - 1)
            for k in range(basis):
                line = taps[pl.ds((slot * basis + k) * rows + i, 1), :] * live
                turned = pltpu.roll(jnp.broadcast_to(line, (LANES, circle)), 0, 1, stride=1, stride_axis=0)
                base[i, pl.ds(k * LANES, LANES), pl.ds(w * circle, circle)] = turned.astype(jnp.bfloat16)
        return carry

    lax.fori_loop(0, rows, build_row, 0)

    take(theta_buf.at[pl.ds(0, L - 1)], th_sem.at[1])
    loads[8].wait()
    scale = jnp.concatenate([theta_buf[owner] for owner in range(L)], axis=1)

    def window(wide, e, i, h):
        cut = h * LANES
        pieces = []
        for w in range(WINDOW):
            pieces.append(wide[e, i + w, pl.ds(cut, circle - cut), :])
            if cut:
                pieces.append(wide[e, i + w, pl.ds(0, cut), :])
        return jnp.concatenate(pieces, axis=0)

    def mixed(prod, scale):
        total = prod[:LANES] * scale[0:1, :]
        for k in range(1, basis):
            total = total + prod[k * LANES:(k + 1) * LANES] * scale[k:k + 1, :]
        return total.astype(jnp.bfloat16)

    latest = jnp.where(lon < L // 2, L // 2, L // 2 - 1)

    def place_of(source, target):
        return lax.rem(source + L - (L // 2 if target < L // 2 else L // 2 - 1), L)

    def head_row(slot, carry):
        i = lax.rem(slot + REACH, rows)
        for e in range(members):
            both = jnp.concatenate([window(wide_a, e, i, h) for h in range(blocks)], axis=1)
            prod = jnp.dot(base[i], both, preferred_element_type=jnp.float32)
            for h in range(blocks):
                staged_a[e, slot, pl.ds(h * LANES, LANES), :] = mixed(
                    prod[:, h * head:(h + 1) * head], scale[:, :head])
            got_a[slot, lax.rem(lon + L - latest, L) * members + e] = staged_a[e, slot, lons(lon), :]
        return carry

    first = max(rows - REACH, 0)
    for step in range(1, L):
        incoming(0, step)
        for side in range(2):
            forward(side, 0, step, owners[step])
    take(held.at[member(0)], local_sem.at[len(pairs)])
    arrived(0, 0)
    lax.fori_loop(0, first, head_row, 0)
    arrived(1, 0)
    lax.fori_loop(first, rows, head_row, 0)

    def back_head(target, e):
        return pltpu.make_async_remote_copy(
            src_ref=staged_a.at[e, :, lons(target), :], dst_ref=got_a.at[:, place_of(lon, target) * members + e],
            send_sem=back_send.at[0], recv_sem=a_recv.at[0],
            device_id={"lon": target}, device_id_type=MESH)

    outward = sorted(range(L), key=lambda p: min(p, L - 1 - p))
    for step in range(1, L):
        incoming(1, step)
        forward(0, 1, step, owners[step])
        if step == 1:
            for target in outward:
                @pl.when(lon != target)
                def _():
                    for e in range(members):
                        back_head(target, e).start()
    for step in range(1, L):
        for c in range(2, len(parts)):
            incoming(c, step)
        forward(1, 1, step, owners[step])
    arrived(0, 1)

    def back(slot, target, e, late):
        return pltpu.make_async_remote_copy(
            src_ref=staged_b.at[e, slot, lons(target), :], dst_ref=got_b.at[slot, place_of(lon, target) * members + e],
            send_sem=back_send.at[0], recv_sem=b_recv.at[slot, 0 if late else 1],
            device_id={"lon": target}, device_id_type=MESH)

    def send_one(slot, target):
        last = L // 2 if target < L // 2 else L // 2 - 1
        for late in (False, True):
            @pl.when((lon == last) if late else (lon != target) & (lon != last))
            def _():
                for e in range(members):
                    back(slot, target, e, late).start()

    lag = [min(BEHIND, rows) if 0 < target < L // 2 else 0 for target in range(L)]

    def send_part(slot, h):
        for target in outward:
            if (target * cols + cols - 1) // LANES == h:
                if lag[target]:
                    @pl.when(slot >= lag[target])
                    def _():
                        send_one(slot - lag[target], target)
                else:
                    send_one(slot, target)

    def conv_row(slot, carry):
        i = lax.rem(slot + REACH, rows)
        for e in range(members):
            for h in range(blocks):
                prod = jnp.dot(base[i], window(wide_b, e, i, h), preferred_element_type=jnp.float32)
                staged_b[e, slot, pl.ds(h * LANES, LANES), :] = mixed(prod, scale[:, head:])
                if e == members - 1 and h > 0:
                    send_part(slot, h - 1)
                if e == 0 and h == 0:
                    @pl.when(slot > 0)
                    def _():
                        send_part(slot - 1, blocks - 1)
            got_b[slot, lax.rem(lon + L - latest, L) * members + e] = staged_b[e, slot, lons(lon), :]
        return carry

    lax.fori_loop(0, first, conv_row, 0)
    arrived(1, 1)
    lax.fori_loop(first, rows, conv_row, 0)
    for copy in loads[3:8]:
        copy.wait()
    take(got_a.at[:, pl.ds(0, (L - 1) * members)], a_recv.at[0])

    def mlp_part(slot, low, high):
        i = lax.rem(slot + REACH, rows)
        fresh = (high - low - min(low, 1)) * members
        if fresh:
            take(got_b.at[slot, pl.ds(0, fresh)], b_recv.at[slot, min(low, 1)])
        count = (high - low) * members
        here = pl.ds(low * members, count)
        branch = channel_mlp(
            got_a[slot, here].reshape(count * cols, head), got_b[slot, here].reshape(count * cols, chans - head),
            gain, w_in, b_in, w_out).reshape(high - low, members, cols, chans)
        for g in range(low, high):
            owned = pl.ds(lax.rem(latest + g, L) * members, members)
            out[owned, i] = (held[owned, i].astype(jnp.float32) + branch[g - low]).astype(jnp.bfloat16)

    def early_row(slot, carry):
        mlp_part(slot, 1, L)

        @pl.when(slot == 0)
        def _():
            send_part(rows - 1, blocks - 1)
            for target in range(L):
                for behind in range(lag[target], 0, -1):
                    send_one(rows - behind, target)

        return carry

    def late_row(slot, carry):
        mlp_part(slot, 0, 1)
        return carry

    lax.fori_loop(0, rows, early_row, 0)
    take(held.at[pl.ds(0, (L - 1) * members)], send_sem.at[0])
    take(theta_buf.at[pl.ds(0, L - 1)], th_sem.at[0])
    for side in range(2):
        @pl.when((has_down, has_up)[side])
        def _():
            take(held.at[:, pl.ds(0, REACH)], halo_send.at[side])
    lax.fori_loop(0, rows - 1, late_row, 0)
    final = (rows - 1 + REACH) % rows
    last_h[...] = held[pl.ds(latest * members, members), final]
    last_a[...] = got_a[rows - 1, pl.ds(0, members)]
    take(got_b.at[rows - 1, pl.ds(0, members)], b_recv.at[rows - 1, 0])
    last_b[...] = got_b[rows - 1, pl.ds(0, members)]
    take(held.at[pl.ds(0, (L - 1) * members)], back_send.at[0])


def block(fields, theta, kern, starts, counts, gain, w_in, b_in, w_out, L, T):
    ens, rows, cols, chans = fields.shape
    members, circle = ens // L, cols * L
    basis = theta.shape[0]
    head = LANES
    tail = chans - head
    dma = pltpu.SemaphoreType.DMA
    bf16 = jnp.bfloat16
    kept = (
        pltpu.VMEM(fields.shape, bf16), pltpu.VMEM((members, cols, head), bf16), pltpu.VMEM((members, cols, tail), bf16),
        pltpu.VMEM((members, cols, chans), bf16), pltpu.VMEM(gain.shape, jnp.float32), pltpu.VMEM(w_in.shape, bf16),
        pltpu.VMEM(b_in.shape, jnp.float32), pltpu.VMEM(w_out.shape, bf16))
    in_vmem = pl.BlockSpec(memory_space=pltpu.VMEM)
    parts = pl.pallas_call(
        functools.partial(block_kernel, L, T, members),
        out_shape=kept,
        in_specs=[pl.BlockSpec(memory_space=pltpu.HBM)] * 9,
        out_specs=[in_vmem] * len(kept),
        scratch_shapes=[
            pltpu.VMEM((members, rows + 2 * REACH, circle, head), bf16),
            pltpu.VMEM((members, rows + 2 * REACH, circle, tail), bf16),
            pltpu.VMEM((rows, basis * LANES, WINDOW * circle), bf16),
            pltpu.VMEM((kern.shape[0] * basis * rows, circle), jnp.float32),
            pltpu.VMEM(kern.shape, jnp.float32),
            pltpu.SMEM(starts.shape, jnp.int32),
            pltpu.SMEM(counts.shape, jnp.int32),
            pltpu.VMEM((L,) + theta.shape, jnp.float32),
            pltpu.VMEM((members, rows, circle, head), bf16),
            pltpu.VMEM((members, rows, circle, tail), bf16),
            pltpu.VMEM((rows, ens, cols, head), bf16),
            pltpu.VMEM((rows, ens, cols, tail), bf16),
            pltpu.VMEM(fields.shape, bf16),
            pltpu.SemaphoreType.REGULAR((2,)), pltpu.SemaphoreType.REGULAR((2,)), dma((1,)), dma((3, L - 1)), dma((2,)), dma((2, 2)), dma((2,)), dma((10,)), dma((1,)), dma((1,)), dma((rows, 2)),
        ],
        compiler_params=pltpu.CompilerParams(
            collective_id=0, has_side_effects=True, vmem_limit_bytes=48 * 2**20),
        name="block",
    )(*(pltpu.with_memory_space_constraint(v, pltpu.HBM)
        for v in (fields, theta, kern, starts, counts, gain, w_in, b_in, w_out)))
    return pl.pallas_call(
        functools.partial(last_kernel, L),
        out_shape=jax.ShapeDtypeStruct(fields.shape, bf16),
        in_specs=[in_vmem] * len(kept),
        out_specs=pl.BlockSpec(memory_space=pltpu.HBM),
        scratch_shapes=[pltpu.VMEM((members, cols, chans), bf16), dma((3,))],
        compiler_params=pltpu.CompilerParams(vmem_limit_bytes=8 * 2**20),
        name="last",
    )(*parts)


def with_halo(value, sides, width):
    for axis, dim in sides:
        size, length = (lax.axis_size(axis), value.shape[dim])
        up = [(i, (i + 1) % size) for i in range(size - 1)]
        down = [(j, i) for i, j in up]
        last = lax.slice_in_dim(value, length - width, length, axis=dim)
        initial = lax.slice_in_dim(value, 0, width, axis=dim)
        before = lax.ppermute(last, axis, up)
        after = lax.ppermute(initial, axis, down)
        value = jnp.concatenate([before, value, after], axis=dim)
    return value


def circle_tables(length):
    bins = length // 2 + 1
    points = jnp.arange(length, dtype=jnp.int32)
    freqs = jnp.arange(bins, dtype=jnp.int32)
    phase = points[:, None] * freqs[None, :] % length
    angle = phase.astype(jnp.float32) * (2.0 * math.pi / length)
    cosine = jnp.cos(angle)
    sine = jnp.sin(angle)
    onward = jnp.concatenate([cosine, -sine], axis=1)
    weight = jnp.where((freqs == 0) | (freqs == length // 2), 1.0, 2.0).astype(jnp.float32)
    backward = (
        jnp.concatenate([(cosine * weight[None, :]).T, (-sine * weight[None, :]).T], axis=0)
        / length
    )
    return (onward, backward, bins)


def forward(field, onward, bins):
    upper = onward.astype(jnp.bfloat16)
    lower = (onward - upper.astype(jnp.float32)).astype(jnp.bfloat16)
    spectrum = jnp.einsum("ejlc,lg->ejgc", field, upper, preferred_element_type=jnp.float32)
    spectrum = spectrum + jnp.einsum(
        "ejlc,lg->ejgc", field, lower, preferred_element_type=jnp.float32
    )
    return (spectrum[:, :, :bins], spectrum[:, :, bins:])


def mix_basis(kern_part, theta):
    mixed = kern_part[:, :, 0, :, None] * theta[0][None, None, None, :]
    for basis in range(1, kern_part.shape[2]):
        mixed = mixed + kern_part[:, :, basis, :, None] * theta[basis][None, None, None, :]
    return mixed


def spectral_shards(fields, kernel, theta, row_start, row_count, norm_gain, w_in, b_in, w_out):
    local = lax.all_to_all(fields, "lon", split_axis=3, concat_axis=2, tiled=True)
    members, band, circle, chans = local.shape
    onward, backward, bins = circle_tables(circle)
    widened = with_halo(local, (("lat", 1),), REACH)
    spec_re, spec_im = forward(widened, onward, bins)
    kern_all = jnp.einsum("irkm,mg->irkg", kernel, onward, precision=lax.Precision.HIGHEST)
    mixed_re = mix_basis(kern_all[..., :bins], theta)
    mixed_im = mix_basis(kern_all[..., bins:], theta)
    first_row = lax.axis_index("lat") * band - REACH
    span_rows = band + 2 * REACH
    slot_ids = jnp.arange(WINDOW, dtype=jnp.int32)
    offsets = row_start - first_row
    live_slot = slot_ids[None, :] < row_count[:, None]
    total_re = jnp.zeros((members, band, bins, chans), jnp.float32)
    total_im = jnp.zeros((members, band, bins, chans), jnp.float32)
    for span in range(span_rows):
        select = (live_slot & (offsets[:, None] + slot_ids[None, :] == span)).astype(jnp.float32)
        coef_re = jnp.einsum("is,isfc->ifc", select, mixed_re, precision=lax.Precision.HIGHEST)
        coef_im = jnp.einsum("is,isfc->ifc", select, mixed_im, precision=lax.Precision.HIGHEST)
        row_re = spec_re[:, span][:, None]
        row_im = spec_im[:, span][:, None]
        total_re = total_re + coef_re * row_re - coef_im * row_im
        total_im = total_im + coef_re * row_im + coef_im * row_re
    joined = jnp.concatenate([total_re, total_im], axis=2)
    conv = jnp.einsum("eigc,gl->eilc", joined, backward, precision=lax.Precision.HIGHEST).astype(
        jnp.bfloat16
    )
    values = lax.all_to_all(conv, "lon", split_axis=2, concat_axis=3, tiled=True).astype(
        jnp.float32
    )
    mean = jnp.mean(values, axis=-1, keepdims=True)
    var = jnp.mean((values - mean) ** 2, axis=-1, keepdims=True)
    normed = ((values - mean) * lax.rsqrt(var + 1e-05) * norm_gain).astype(jnp.bfloat16)
    hidden = jax.nn.gelu(
        jnp.einsum("eblc,ch->eblh", normed, w_in, preferred_element_type=jnp.float32) + b_in,
        approximate=False,
    ).astype(jnp.bfloat16)
    branch = jnp.einsum("eblh,hc->eblc", hidden, w_out, preferred_element_type=jnp.float32)
    return (fields.astype(jnp.float32) + branch).astype(jnp.bfloat16)


def shards(L, T, fields, kernel, theta, row_start, row_count, norm_gain, w_in, b_in, w_out):
    if L == 1 or fields.shape[0] % L:
        return spectral_shards(
            fields, kernel, theta, row_start, row_count, norm_gain, w_in, b_in, w_out
        )
    kern = jnp.transpose(kernel, (1, 2, 0, 3))
    return block(fields, theta, kern, row_start, row_count, norm_gain, w_in, b_in, w_out, L, T)


def solution(mesh):
    placed = (
        P(None, "lat", "lon", None),
        P("lat", None, None, None),
        P(None, "lon"),
        P("lat"),
        P("lat"),
        P(),
        P(),
        P(),
        P(),
    )
    return jax.shard_map(
        functools.partial(shards, mesh.shape["lon"], mesh.shape["lat"]),
        mesh=mesh, in_specs=placed, out_specs=P(None, "lat", "lon", None), check_vma=False,
    )
```

```python
import functools
import math

import jax
import jax.numpy as jnp
from jax import lax
from jax.experimental import pallas as pl
from jax.experimental.pallas import tpu as pltpu
from jax.sharding import PartitionSpec as P

REACH = 4
WINDOW = 2 * REACH + 1
LANES = 128
BEHIND = 2
MESH = pl.DeviceIdType.MESH


def channel_mlp(first, rest, gain, w_in, b_in, w_out):
    values = jnp.concatenate([first, rest], axis=1).astype(jnp.float32)
    mean = jnp.mean(values, axis=-1, keepdims=True)
    diff = values - mean
    var = jnp.mean(diff * diff, axis=-1, keepdims=True)
    normed = (diff * lax.rsqrt(var + 1e-05) * gain[...][None, :]).astype(jnp.bfloat16)
    hidden = jnp.dot(normed, w_in[...], preferred_element_type=jnp.float32) + b_in[...][None, :]
    hidden = (0.5 * hidden * (1.0 + lax.erf(hidden * math.sqrt(0.5)))).astype(jnp.bfloat16)
    return jnp.dot(hidden, w_out[...], preferred_element_type=jnp.float32)


def last_kernel(L, done, last_a, last_b, last_h, gain, w_in, b_in, w_out, out, piece, sem):
    lon = lax.axis_index("lon")
    ens, rows, cols, chans = out.shape
    members, _, head = last_a.shape
    latest = jnp.where(lon < L // 2, L // 2, L // 2 - 1)
    final = (rows - 1 + REACH) % rows
    for e in range(ens):
        pltpu.make_async_copy(done.at[e, final + 1:], out.at[e, final + 1:], sem.at[0]).start()
        if e < ens // 2:
            pltpu.make_async_copy(done.at[e, :final], out.at[e, :final], sem.at[0]).start()
    branch = channel_mlp(
        last_a[...].reshape(members * cols, head), last_b[...].reshape(members * cols, chans - head),
        gain, w_in, b_in, w_out).reshape(members, cols, chans)
    piece[...] = (last_h[...].astype(jnp.float32) + branch).astype(jnp.bfloat16)
    copy = pltpu.make_async_copy(piece, out.at[pl.ds(latest * members, members), final], sem.at[1])
    copy.start()
    for e in range(ens // 2, ens):
        pltpu.make_async_copy(done.at[e, :final], out.at[e, :final], sem.at[0]).start()
    for g in range(1, L):
        owned = pl.ds(lax.rem(latest + g, L) * members, members)
        pltpu.make_async_copy(done.at[owned, final], out.at[owned, final], sem.at[2]).start()
    if rows > 1:
        pltpu.make_async_copy(done.at[:, :rows - 1], out.at[:, :rows - 1], sem.at[0]).wait()
    pltpu.make_async_copy(done.at[:ens - members, 0], out.at[:ens - members, 0], sem.at[2]).wait()
    copy.wait()


def block_kernel(
    L, T, members, fields, theta, kern_hbm, starts_hbm, counts_hbm, gain_hbm, w_in_hbm, b_in_hbm, w_out_hbm,
    out, last_a, last_b, last_h, gain, w_in, b_in, w_out,
    wide_a, wide_b, base, taps, kern, starts, counts, theta_buf,
    staged_a, staged_b, got_a, got_b, held,
    far_sem, lat_sem, send_sem, recv_sem, halo_send, halo_recv, th_sem, local_sem, back_send, a_recv, early_recv, late_recv, first_recv,
):
    lat, lon = lax.axis_index("lat"), lax.axis_index("lon")
    up, down = lax.rem(lat + 1, T), lax.rem(lat + T - 1, T)
    has_up, has_down = lat < T - 1, lat > 0
    ens, rows, cols, chans = held.shape
    circle = wide_a.shape[2]
    slots, basis = kern.shape[:2]
    head = wide_a.shape[3]
    blocks = circle // LANES
    pair = 2 - rows % 2
    pooled = max(rows // 2 - 1, 0)

    pairs = ((kern_hbm, kern), (starts_hbm, starts), (counts_hbm, counts), (gain_hbm, gain),
             (w_in_hbm, w_in), (b_in_hbm, b_in), (w_out_hbm, w_out), (fields, held), (theta, theta_buf.at[lon]))
    loads = [pltpu.make_async_copy(a, b, local_sem.at[n]) for n, (a, b) in enumerate(pairs)]
    barrier = pltpu.get_barrier_semaphore()
    half = L // 2
    low = lon < half
    inward, outward_by = jnp.where(low, lon + 1, lon - 1), jnp.where(low, lon - 1, lon + 1)
    middle = (lon == half - 1) | (lon == half)
    at_end = (lon == 0) | (lon == L - 1)
    relayed = ((lon == 1) | (lon == L - 2)) if L > 3 else lon < 0
    beside = ((down, has_down), (up, has_up))

    def signal(sem, when, **device):
        @pl.when(when)
        def _():
            pl.semaphore_signal(sem, inc=1, device_id=device, device_id_type=MESH)

    signal(barrier, ~at_end, lon=outward_by)
    signal(barrier, middle, lon=inward)
    for other, there in beside:
        signal(barrier, there & ~relayed, lat=other)
    greeted = [jnp.where(there & ~relayed, 1, 0) for _, there in beside]
    pl.semaphore_wait(barrier, 1 + greeted[0] + greeted[1])

    def learn(side, when):
        @pl.when(when)
        def _():
            pl.semaphore_wait(far_sem.at[side], 1)

    def take(ref, sem):
        pltpu.make_async_copy(ref, ref, sem).wait()

    owners = [lax.rem(lon + L - step, L) for step in range(L)]

    def lons(owner):
        return pl.ds(pl.multiple_of(owner * cols, cols), cols)

    def member(owner):
        return pl.ds(owner * members, members)

    parts = [(wide_a, pl.ds(0, head), 0, rows), (wide_b, pl.ds(head, chans - head), 0, REACH)]
    if rows > REACH:
        parts.append((wide_b, pl.ds(head, chans - head), REACH, rows - REACH))
    def send_theta(peer):
        pltpu.make_async_remote_copy(
            src_ref=theta, dst_ref=theta_buf.at[lon], send_sem=th_sem.at[0], recv_sem=th_sem.at[1],
            device_id={"lon": peer}, device_id_type=MESH).start()

    def outgoing(c, peer):
        wide, chan, low, size = parts[c]
        return pltpu.make_async_remote_copy(
            src_ref=fields.at[member(peer), pl.ds(low, size), :, chan],
            dst_ref=wide.at[:, pl.ds(REACH + low, size), lons(lon), :],
            send_sem=send_sem.at[0], recv_sem=recv_sem.at[c - 1, lax.rem(peer - lon + L, L) - 1] if c else first_recv.at[0],
            device_id={"lon": peer}, device_id_type=MESH)

    def incoming(c, step):
        wide, chan, low, size = parts[c]
        take(wide.at[:, pl.ds(REACH + low, size), lons(owners[step]), :], recv_sem.at[c - 1, step - 1])

    def both_ways(distance, act):
        for peer, known in ((lon - distance, lon >= distance), (lon + distance, lon + distance < L)):
            pl.when(known)(functools.partial(act, peer))

    def begin(peer):
        outgoing(0, peer).start()
        send_theta(peer)

    begin(inward)
    signal(far_sem.at[1], ~middle, lon=inward)
    for copy in loads[:3]:
        copy.start()
    for side, (other, there) in enumerate(beside):
        signal(lat_sem.at[1 - side], there & at_end & (L > 3), lat=other)
    inner_count = jnp.where(low, L - 1 - lon, lon)
    outer_count = L - 1 - inner_count
    for distance in range(1, L):
        known = distance <= outer_count
        learn(1, known)
        signal(far_sem.at[1], known & ~middle, lon=inward)
        if distance == 1:
            signal(far_sem.at[0], known, lon=outward_by)
            signal(far_sem.at[0], known & middle, lon=inward)
        else:
            signal(far_sem.at[0], known & middle, lon=inward)
        pl.when(known)(functools.partial(begin, jnp.where(low, lon - distance, lon + distance)))
        if distance > 1:
            known = distance <= inner_count
            learn(0, known)
            signal(far_sem.at[0], known & ~at_end, lon=outward_by)
            pl.when(known)(functools.partial(begin, jnp.where(low, lon + distance, lon - distance)))
    for side, (other, there) in enumerate(beside):
        @pl.when(there & (at_end | relayed) & (L > 3))
        def _():
            pl.semaphore_wait(lat_sem.at[side], 1)

        signal(lat_sem.at[side], there & at_end & (L > 3), lon=inward)
    for c in range(1, len(parts)):
        for distance in range(1, L):
            both_ways(distance, lambda peer: outgoing(c, peer).start())
    mine = [
        pltpu.make_async_copy(
            fields.at[member(lon), :, :, chan], wide.at[:, pl.ds(REACH, rows), lons(lon), :], local_sem.at[len(pairs)])
        for wide, chan, _, _ in parts[:2]]
    for copy in mine + loads[3:]:
        copy.start()

    def forward(side, part, step, owner):
        wide, chan = parts[part][:2]
        source, target, other, there = ((0, REACH + rows, down, has_down), (rows - REACH, 0, up, has_up))[side]
        if step:
            src = wide.at[:, pl.ds(REACH + source, REACH), lons(owner), :]
        else:
            src = fields.at[member(owner), pl.ds(source, REACH), :, chan]
        copy = pltpu.make_async_remote_copy(
            src_ref=src, dst_ref=wide.at[:, pl.ds(target, REACH), lons(owner), :],
            send_sem=halo_send.at[side], recv_sem=halo_recv.at[side, part],
            device_id={"lat": other}, device_id_type=MESH)
        pl.when(there)(copy.start)

    def arrived(side, part):
        @pl.when((has_up, has_down)[side])
        def _():
            target = (REACH + rows, 0)[side]
            take(parts[part][0].at[:, pl.ds(target, REACH)], halo_recv.at[side, part])

    for side in range(2):
        for part in range(2):
            forward(side, part, 0, lon)

    @pl.when(lat == 0)
    def _():
        for wide in (wide_a, wide_b):
            wide[:, :REACH] = jnp.zeros_like(wide[:, :REACH])

    @pl.when(lat == T - 1)
    def _():
        for wide in (wide_a, wide_b):
            wide[:, REACH + rows:] = jnp.zeros_like(wide[:, REACH + rows:])

    place = lax.broadcasted_iota(jnp.int32, (circle, circle), 0) + lax.broadcasted_iota(
        jnp.int32, (circle, circle), 1)
    flip = jnp.where((place == 0) | (place == circle), 1.0, 0.0).astype(jnp.bfloat16)

    for copy in loads[:3]:
        copy.wait()
    profiles = kern[...].reshape(slots * basis * rows, circle).astype(jnp.bfloat16)
    taps[...] = jnp.dot(profiles, flip, preferred_element_type=jnp.float32)

    def build_row(i, carry):
        shift = starts[i] - (lat * rows + i - REACH)
        count = counts[i]
        for w in range(WINDOW):
            slot = w - shift
            live = jnp.where((slot >= 0) & (slot < count), 1.0, 0.0)
            slot = jnp.clip(slot, 0, slots - 1)
            for k in range(basis):
                line = taps[pl.ds((slot * basis + k) * rows + i, 1), :] * live
                turned = pltpu.roll(jnp.broadcast_to(line, (LANES, circle)), 0, 1, stride=1, stride_axis=0)
                base[i, pl.ds(k * LANES, LANES), pl.ds(w * circle, circle)] = turned.astype(jnp.bfloat16)
        return carry

    lax.fori_loop(0, rows, build_row, 0)

    take(theta_buf.at[pl.ds(0, L - 1)], th_sem.at[1])
    loads[8].wait()
    scale = jnp.concatenate([theta_buf[owner] for owner in range(L)], axis=1)

    def window(wide, e, i, h):
        cut = h * LANES
        pieces = []
        for w in range(WINDOW):
            pieces.append(wide[e, i + w, pl.ds(cut, circle - cut), :])
            if cut:
                pieces.append(wide[e, i + w, pl.ds(0, cut), :])
        return jnp.concatenate(pieces, axis=0)

    def mixed(prod, scale):
        total = prod[:LANES] * scale[0:1, :]
        for k in range(1, basis):
            total = total + prod[k * LANES:(k + 1) * LANES] * scale[k:k + 1, :]
        return total.astype(jnp.bfloat16)

    latest = jnp.where(lon < L // 2, L // 2, L // 2 - 1)

    def place_of(source, target):
        return lax.rem(source + L - (L // 2 if target < L // 2 else L // 2 - 1), L)

    def head_row(slot, carry):
        i = lax.rem(slot + REACH, rows)
        for e in range(members):
            both = jnp.concatenate([window(wide_a, e, i, h) for h in range(blocks)], axis=1)
            prod = jnp.dot(base[i], both, preferred_element_type=jnp.float32)
            for h in range(blocks):
                staged_a[e, slot, pl.ds(h * LANES, LANES), :] = mixed(
                    prod[:, h * head:(h + 1) * head], scale[:, :head])
            got_a[slot, lax.rem(lon + L - latest, L) * members + e] = staged_a[e, slot, lons(lon), :]
        return carry

    first = max(rows - REACH, 0)
    take(got_a.at[:, pl.ds(0, (L - 1) * members)], first_recv.at[0])
    for step in range(1, L):
        for side in range(2):
            forward(side, 0, step, owners[step])
    take(held.at[member(0)], local_sem.at[len(pairs)])
    arrived(0, 0)
    lax.fori_loop(0, first, head_row, 0)
    arrived(1, 0)
    lax.fori_loop(first, rows, head_row, 0)

    def back_head(target, e):
        return pltpu.make_async_remote_copy(
            src_ref=staged_a.at[e, :, lons(target), :], dst_ref=got_a.at[:, place_of(lon, target) * members + e],
            send_sem=back_send.at[0], recv_sem=a_recv.at[0],
            device_id={"lon": target}, device_id_type=MESH)

    outward = sorted(range(L), key=lambda p: min(p, L - 1 - p))
    for step in range(1, L):
        incoming(1, step)
        forward(0, 1, step, owners[step])
        if step == 1:
            for target in outward:
                @pl.when(lon != target)
                def _():
                    for e in range(members):
                        back_head(target, e).start()
    for step in range(1, L):
        for c in range(2, len(parts)):
            incoming(c, step)
        forward(1, 1, step, owners[step])
    arrived(0, 1)

    def back(slot, target, e, late):
        return pltpu.make_async_remote_copy(
            src_ref=staged_b.at[e, slot, lons(target), :], dst_ref=got_b.at[slot, place_of(lon, target) * members + e],
            send_sem=back_send.at[0], recv_sem=late_recv.at[jnp.maximum(slot - pooled, 0)] if late else early_recv.at[slot // pair],
            device_id={"lon": target}, device_id_type=MESH)

    def send_one(slot, target):
        last = L // 2 if target < L // 2 else L // 2 - 1
        for late in (False, True):
            @pl.when((lon == last) if late else (lon != target) & (lon != last))
            def _():
                for e in range(members):
                    back(slot, target, e, late).start()

    lag = [min(BEHIND, rows) if 0 < target < L // 2 else 0 for target in range(L)]

    def send_part(slot, h):
        for target in outward:
            if (target * cols + cols - 1) // LANES == h:
                if lag[target]:
                    @pl.when(slot >= lag[target])
                    def _():
                        send_one(slot - lag[target], target)
                else:
                    send_one(slot, target)

    def conv_row(slot, carry):
        i = lax.rem(slot + REACH, rows)
        for e in range(members):
            for h in range(blocks):
                prod = jnp.dot(base[i], window(wide_b, e, i, h), preferred_element_type=jnp.float32)
                staged_b[e, slot, pl.ds(h * LANES, LANES), :] = mixed(prod, scale[:, head:])
                if e == members - 1 and h > 0:
                    send_part(slot, h - 1)
                if e == 0 and h == 0:
                    @pl.when(slot > 0)
                    def _():
                        send_part(slot - 1, blocks - 1)
            got_b[slot, lax.rem(lon + L - latest, L) * members + e] = staged_b[e, slot, lons(lon), :]
        return carry

    lax.fori_loop(0, first, conv_row, 0)
    arrived(1, 1)
    lax.fori_loop(first, rows, conv_row, 0)
    for copy in loads[3:8]:
        copy.wait()
    take(got_a.at[:, pl.ds(0, (L - 1) * members)], a_recv.at[0])

    def mlp_part(slot, low, high):
        i = lax.rem(slot + REACH, rows)
        fresh = (high - low - min(low, 1)) * members
        if fresh and low:
            @pl.when(slot % pair == 0)
            def _():
                take(got_b.at[pl.ds(slot, pair), pl.ds(0, fresh)], early_recv.at[slot // pair])
        elif fresh:
            @pl.when(slot > pooled)
            def _():
                take(got_b.at[slot, pl.ds(0, fresh)], late_recv.at[slot - pooled])
        count = (high - low) * members
        here = pl.ds(low * members, count)
        branch = channel_mlp(
            got_a[slot, here].reshape(count * cols, head), got_b[slot, here].reshape(count * cols, chans - head),
            gain, w_in, b_in, w_out).reshape(high - low, members, cols, chans)
        for g in range(low, high):
            owned = pl.ds(lax.rem(latest + g, L) * members, members)
            out[owned, i] = (held[owned, i].astype(jnp.float32) + branch[g - low]).astype(jnp.bfloat16)

    def early_row(slot, carry):
        mlp_part(slot, 1, L)

        @pl.when(slot == 0)
        def _():
            send_part(rows - 1, blocks - 1)
            for target in range(L):
                for behind in range(lag[target], 0, -1):
                    send_one(rows - behind, target)

        return carry

    def late_row(slot, carry):
        mlp_part(slot, 0, 1)
        return carry

    lax.fori_loop(0, rows, early_row, 0)
    take(held.at[pl.ds(0, (L - 1) * members)], send_sem.at[0])
    take(theta_buf.at[pl.ds(0, L - 1)], th_sem.at[0])
    for side in range(2):
        @pl.when((has_down, has_up)[side])
        def _():
            take(held.at[:, pl.ds(0, REACH)], halo_send.at[side])
    take(got_b.at[pl.ds(0, pooled + 1), pl.ds(0, members)], late_recv.at[0])
    lax.fori_loop(0, rows - 1, late_row, 0)
    final = (rows - 1 + REACH) % rows
    last_h[...] = held[pl.ds(latest * members, members), final]
    last_a[...] = got_a[rows - 1, pl.ds(0, members)]
    take(got_b.at[rows - 1, pl.ds(0, members)], late_recv.at[rows - 1 - pooled])
    last_b[...] = got_b[rows - 1, pl.ds(0, members)]
    take(held.at[pl.ds(0, (L - 1) * members)], back_send.at[0])


def block(fields, theta, kern, starts, counts, gain, w_in, b_in, w_out, L, T):
    ens, rows, cols, chans = fields.shape
    members, circle = ens // L, cols * L
    basis = theta.shape[0]
    head = LANES
    tail = chans - head
    dma = pltpu.SemaphoreType.DMA
    bf16 = jnp.bfloat16
    kept = (
        pltpu.VMEM(fields.shape, bf16), pltpu.VMEM((members, cols, head), bf16), pltpu.VMEM((members, cols, tail), bf16),
        pltpu.VMEM((members, cols, chans), bf16), pltpu.VMEM(gain.shape, jnp.float32), pltpu.VMEM(w_in.shape, bf16),
        pltpu.VMEM(b_in.shape, jnp.float32), pltpu.VMEM(w_out.shape, bf16))
    in_vmem = pl.BlockSpec(memory_space=pltpu.VMEM)
    parts = pl.pallas_call(
        functools.partial(block_kernel, L, T, members),
        out_shape=kept,
        in_specs=[pl.BlockSpec(memory_space=pltpu.HBM)] * 9,
        out_specs=[in_vmem] * len(kept),
        scratch_shapes=[
            pltpu.VMEM((members, rows + 2 * REACH, circle, head), bf16),
            pltpu.VMEM((members, rows + 2 * REACH, circle, tail), bf16),
            pltpu.VMEM((rows, basis * LANES, WINDOW * circle), bf16),
            pltpu.VMEM((kern.shape[0] * basis * rows, circle), jnp.float32),
            pltpu.VMEM(kern.shape, jnp.float32),
            pltpu.SMEM(starts.shape, jnp.int32),
            pltpu.SMEM(counts.shape, jnp.int32),
            pltpu.VMEM((L,) + theta.shape, jnp.float32),
            pltpu.VMEM((members, rows, circle, head), bf16),
            pltpu.VMEM((members, rows, circle, tail), bf16),
            pltpu.VMEM((rows, ens, cols, head), bf16),
            pltpu.VMEM((rows, ens, cols, tail), bf16),
            pltpu.VMEM(fields.shape, bf16),
            pltpu.SemaphoreType.REGULAR((2,)), pltpu.SemaphoreType.REGULAR((2,)), dma((1,)), dma((2, L - 1)), dma((2,)), dma((2, 2)), dma((2,)), dma((10,)), dma((1,)), dma((1,)), dma((rows,) if rows % 2 else (rows // 2,)),
            dma((rows - max(rows // 2 - 1, 0),)), dma((1,)),
        ],
        compiler_params=pltpu.CompilerParams(
            collective_id=0, has_side_effects=True, vmem_limit_bytes=48 * 2**20),
        name="block",
    )(*(pltpu.with_memory_space_constraint(v, pltpu.HBM)
        for v in (fields, theta, kern, starts, counts, gain, w_in, b_in, w_out)))
    return pl.pallas_call(
        functools.partial(last_kernel, L),
        out_shape=jax.ShapeDtypeStruct(fields.shape, bf16),
        in_specs=[in_vmem] * len(kept),
        out_specs=pl.BlockSpec(memory_space=pltpu.HBM),
        scratch_shapes=[pltpu.VMEM((members, cols, chans), bf16), dma((3,))],
        compiler_params=pltpu.CompilerParams(vmem_limit_bytes=8 * 2**20),
        name="last",
    )(*parts)


def with_halo(value, sides, width):
    for axis, dim in sides:
        size, length = (lax.axis_size(axis), value.shape[dim])
        up = [(i, (i + 1) % size) for i in range(size - 1)]
        down = [(j, i) for i, j in up]
        last = lax.slice_in_dim(value, length - width, length, axis=dim)
        initial = lax.slice_in_dim(value, 0, width, axis=dim)
        before = lax.ppermute(last, axis, up)
        after = lax.ppermute(initial, axis, down)
        value = jnp.concatenate([before, value, after], axis=dim)
    return value


def circle_tables(length):
    bins = length // 2 + 1
    points = jnp.arange(length, dtype=jnp.int32)
    freqs = jnp.arange(bins, dtype=jnp.int32)
    phase = points[:, None] * freqs[None, :] % length
    angle = phase.astype(jnp.float32) * (2.0 * math.pi / length)
    cosine = jnp.cos(angle)
    sine = jnp.sin(angle)
    onward = jnp.concatenate([cosine, -sine], axis=1)
    weight = jnp.where((freqs == 0) | (freqs == length // 2), 1.0, 2.0).astype(jnp.float32)
    backward = (
        jnp.concatenate([(cosine * weight[None, :]).T, (-sine * weight[None, :]).T], axis=0)
        / length
    )
    return (onward, backward, bins)


def forward(field, onward, bins):
    upper = onward.astype(jnp.bfloat16)
    lower = (onward - upper.astype(jnp.float32)).astype(jnp.bfloat16)
    spectrum = jnp.einsum("ejlc,lg->ejgc", field, upper, preferred_element_type=jnp.float32)
    spectrum = spectrum + jnp.einsum(
        "ejlc,lg->ejgc", field, lower, preferred_element_type=jnp.float32
    )
    return (spectrum[:, :, :bins], spectrum[:, :, bins:])


def mix_basis(kern_part, theta):
    mixed = kern_part[:, :, 0, :, None] * theta[0][None, None, None, :]
    for basis in range(1, kern_part.shape[2]):
        mixed = mixed + kern_part[:, :, basis, :, None] * theta[basis][None, None, None, :]
    return mixed


def spectral_shards(fields, kernel, theta, row_start, row_count, norm_gain, w_in, b_in, w_out):
    local = lax.all_to_all(fields, "lon", split_axis=3, concat_axis=2, tiled=True)
    members, band, circle, chans = local.shape
    onward, backward, bins = circle_tables(circle)
    widened = with_halo(local, (("lat", 1),), REACH)
    spec_re, spec_im = forward(widened, onward, bins)
    kern_all = jnp.einsum("irkm,mg->irkg", kernel, onward, precision=lax.Precision.HIGHEST)
    mixed_re = mix_basis(kern_all[..., :bins], theta)
    mixed_im = mix_basis(kern_all[..., bins:], theta)
    first_row = lax.axis_index("lat") * band - REACH
    span_rows = band + 2 * REACH
    slot_ids = jnp.arange(WINDOW, dtype=jnp.int32)
    offsets = row_start - first_row
    live_slot = slot_ids[None, :] < row_count[:, None]
    total_re = jnp.zeros((members, band, bins, chans), jnp.float32)
    total_im = jnp.zeros((members, band, bins, chans), jnp.float32)
    for span in range(span_rows):
        select = (live_slot & (offsets[:, None] + slot_ids[None, :] == span)).astype(jnp.float32)
        coef_re = jnp.einsum("is,isfc->ifc", select, mixed_re, precision=lax.Precision.HIGHEST)
        coef_im = jnp.einsum("is,isfc->ifc", select, mixed_im, precision=lax.Precision.HIGHEST)
        row_re = spec_re[:, span][:, None]
        row_im = spec_im[:, span][:, None]
        total_re = total_re + coef_re * row_re - coef_im * row_im
        total_im = total_im + coef_re * row_im + coef_im * row_re
    joined = jnp.concatenate([total_re, total_im], axis=2)
    conv = jnp.einsum("eigc,gl->eilc", joined, backward, precision=lax.Precision.HIGHEST).astype(
        jnp.bfloat16
    )
    values = lax.all_to_all(conv, "lon", split_axis=2, concat_axis=3, tiled=True).astype(
        jnp.float32
    )
    mean = jnp.mean(values, axis=-1, keepdims=True)
    var = jnp.mean((values - mean) ** 2, axis=-1, keepdims=True)
    normed = ((values - mean) * lax.rsqrt(var + 1e-05) * norm_gain).astype(jnp.bfloat16)
    hidden = jax.nn.gelu(
        jnp.einsum("eblc,ch->eblh", normed, w_in, preferred_element_type=jnp.float32) + b_in,
        approximate=False,
    ).astype(jnp.bfloat16)
    branch = jnp.einsum("eblh,hc->eblc", hidden, w_out, preferred_element_type=jnp.float32)
    return (fields.astype(jnp.float32) + branch).astype(jnp.bfloat16)


def shards(L, T, fields, kernel, theta, row_start, row_count, norm_gain, w_in, b_in, w_out):
    if L == 1 or fields.shape[0] % L:
        return spectral_shards(
            fields, kernel, theta, row_start, row_count, norm_gain, w_in, b_in, w_out
        )
    kern = jnp.transpose(kernel, (1, 2, 0, 3))
    return block(fields, theta, kern, row_start, row_count, norm_gain, w_in, b_in, w_out, L, T)


def solution(mesh):
    placed = (
        P(None, "lat", "lon", None),
        P("lat", None, None, None),
        P(None, "lon"),
        P("lat"),
        P("lat"),
        P(),
        P(),
        P(),
        P(),
    )
    return jax.shard_map(
        functools.partial(shards, mesh.shape["lon"], mesh.shape["lat"]),
        mesh=mesh, in_specs=placed, out_specs=P(None, "lat", "lon", None), check_vma=False,
    )
```
